32 devices in a mesh: mode: 8 (over z, x), space: 4 (over y, core).
Axes of the slice: x: 2, y: 2, z: 4, core: 2. Of those that a mesh axis runs over, the one named last changes fastest.
Arguments:
- forcing: float32 [64, 64, 256], P('mode', 'space'), may hold values from -8 to 8
- mean_field: float32 [64, 256], P('space'), may hold values from 0.5 to 2
- coef_fields: float32 [28, 64, 256], P(None, 'space'), may hold values from -3 to 3
- color: int32 [64], replicated, may hold values from 0 to 3, as said below
- pair_src: int32 [4, 64, 24], P(None, 'mode'), may hold values from 0 to 63, as said below
- pair_field: int32 [4, 64, 24], P(None, 'mode'), may hold values from 0 to 27
- pair_value: float32 [4, 64, 24], P(None, 'mode'), may hold values from -1.25 to 1.25
Outputs:
- solution: float32 [64, 64, 256], P('mode', 'space')
- residual: float32 [64, 64, 256], P('mode', 'space')
The draws below stay inside these ranges and needn't reach their ends.
Inputs may be any that keep to these rules, and one draw needn't show every extreme that they name: `color`: every aligned block of 8 modes holds exactly 2 modes of each batch. `pair_src`: the entries of batch c name only modes whose color is c.
All inputs are finite; a program needn't handle non-finite values.
Results may differ from the reference program's by a relative error of at most 0.0001.
Values sent between devices are 32-bit elements; how exact they have to be, the bound alone decides.
A program may use at most 64 MiB of HBM per device.

```python
import math
import jax
import jax.numpy as jnp
from jax import lax

NZ = 24
MODE_DEV = 8
NB = 4
SWEEPS = 2
K = 28
MODES = 64
NX = 64
NY = 256


def make_colors(key):
    blocks = MODES // MODE_DEV
    block_keys = jax.random.split(jax.random.fold_in(key, 11), blocks)
    orders = jax.vmap(lambda block_key: jax.random.permutation(block_key, MODE_DEV))(block_keys)
    return (orders % NB).reshape(-1).astype(jnp.int32)


def draw_color(key, part):
    return make_colors(key)


def draw_pair_src(key, part):
    colors = make_colors(key)
    blocks = MODES // MODE_DEV
    per_batch = MODE_DEV // NB
    grouped = colors.reshape(blocks, MODE_DEV)
    onehot = (grouped[:, :, None] == jnp.arange(NB, dtype=jnp.int32)[None, None, :]).astype(jnp.int32)
    earlier = jnp.cumsum(onehot, axis=1) - onehot
    ranking = jnp.sum(onehot * earlier, axis=2).reshape(-1)
    owners = jnp.arange(MODES, dtype=jnp.int32) // MODE_DEV
    lookup = jnp.zeros((blocks * NB * per_batch,), jnp.int32)
    lookup = lookup.at[owners * NB * per_batch + colors * per_batch + ranking].set(jnp.arange(MODES, dtype=jnp.int32))
    device_ids = jax.random.randint(jax.random.fold_in(key, 23), (NB, MODES, NZ), 0, blocks)
    slot_ids = jax.random.randint(jax.random.fold_in(key, 29), (NB, MODES, NZ), 0, per_batch)
    batch_ids = jnp.arange(NB, dtype=jnp.int32)[:, None, None]
    return jnp.take(lookup, device_ids * NB * per_batch + batch_ids * per_batch + slot_ids).astype(jnp.int32)


def set_ends(values, stream_key, smallest, high):
    longest = values.shape.index(max(values.shape))
    spots = []
    for shift in (0, 1):
        where = [jax.random.randint(jax.random.fold_in(stream_key, axis), (), 0, length) for axis, length in enumerate(values.shape)]
        where[longest] = (where[longest] + shift) % values.shape[longest]
        spots.append(tuple(where))
    return values.at[spots[0]].set(smallest).at[spots[1]].set(high)


def block_scale(rng, shape, pieces, least, largest):
    gain = 1.0
    for axis_at, blocks in pieces:
        draws = jax.random.uniform(jax.random.fold_in(jax.random.fold_in(rng, 6), axis_at), (blocks,), jnp.float32, least / len(pieces), largest / len(pieces))
        gain = gain * jnp.repeat(jnp.exp(draws), shape[axis_at] // blocks).reshape((-1,) + (1,) * (len(shape) - 1 - axis_at))
    return gain


def scatter_about(stream_key, extent, scale, most, pieces=(), held_as=jnp.bfloat16):
    level = block_scale(stream_key, extent, pieces, -0.22, 0.18) if pieces else 1.0
    array = jax.random.normal(stream_key, extent, jnp.float32) * scale * level
    return jnp.minimum(jnp.maximum(array, -most), most).astype(held_as)


def setup_inputs(seed: int = 0) -> dict:
    keys = jax.random.split(jax.random.key(seed), 8)
    forcing = scatter_about(keys[0], (MODES, NX, NY), 1.0, 8.0, ((0, 8), (1, 4)), jnp.float32)
    mean_field = jnp.clip(jnp.exp(math.log(2.0) - 1.3862944 * jax.random.uniform(keys[1], (NX, NY), jnp.float32) ** block_scale(keys[1], (NX, NY), ((0, 4),), -0.2, 0.2)), 0.5, 2.0)
    coef_fields = scatter_about(keys[2], (K, NX, NY), 0.5, 3.0, ((1, 4),), jnp.float32)
    color = draw_color(jax.random.fold_in(keys[7], 71), 0)
    pair_src = draw_pair_src(jax.random.fold_in(keys[7], 71), 0)
    pair_field = set_ends(jax.random.randint(keys[5], (NB, MODES, NZ), 0, K), jax.random.fold_in(keys[5], 1), 0, K - 1).astype(jnp.int32)
    pair_value = scatter_about(keys[6], (NB, MODES, NZ), NZ ** -0.5, 1.25, ((1, 8),), jnp.float32)
    return dict(forcing=forcing, mean_field=mean_field, coef_fields=coef_fields, color=color, pair_src=pair_src, pair_field=pair_field, pair_value=pair_value)


def stencil(coeff_field, values):
    height, breadth = coeff_field.shape
    coeff_pad = jnp.pad(coeff_field, ((1, 1), (1, 1)))
    value_pad = jnp.pad(values, ((1, 1), (1, 1)))
    result = jnp.zeros((height, breadth), jnp.float32)
    for step_x, step_y in ((1, 0), (-1, 0), (0, 1), (0, -1)):
        coeff_near = coeff_pad[1 + step_x:1 + step_x + height, 1 + step_y:1 + step_y + breadth]
        value_near = value_pad[1 + step_x:1 + step_x + height, 1 + step_y:1 + step_y + breadth]
        result = result + 0.5 * (coeff_field + coeff_near) * (values - value_near)
    return result


def face_sum(coeff_field):
    height, breadth = coeff_field.shape
    coeff_pad = jnp.pad(coeff_field, ((1, 1), (1, 1)))
    result = jnp.zeros((height, breadth), jnp.float32)
    for step_x, step_y in ((1, 0), (-1, 0), (0, 1), (0, -1)):
        coeff_near = coeff_pad[1 + step_x:1 + step_x + height, 1 + step_y:1 + step_y + breadth]
        result = result + 0.5 * (coeff_field + coeff_near)
    return result


def couple(update, sources, field_ids, weights, coef_fields):
    def reader(reader_entry):
        source_rows, field_rows, weight_rows = reader_entry
        values = jnp.take(update, source_rows, axis=0)
        coeffs = jnp.take(coef_fields, field_rows, axis=0)
        fluxes = jax.vmap(stencil)(coeffs, values)
        return jnp.sum(weight_rows[:, None, None] * fluxes, axis=0)
    return lax.map(reader, (sources, field_ids, weights))


def reference(forcing, mean_field, coef_fields, color, pair_src, pair_field, pair_value):
    diag_sum = face_sum(mean_field)
    solution = jnp.zeros(forcing.shape, jnp.float32)
    coupled = jnp.zeros(forcing.shape, jnp.float32)
    for sweep_idx in range(SWEEPS):
        for color_idx in range(NB):
            active = (color == color_idx)[:, None, None]
            update = jnp.where(active, (forcing - coupled) / diag_sum, 0.0)
            solution = solution + update
            coupled = coupled + couple(update, pair_src[color_idx], pair_field[color_idx], pair_value[color_idx], coef_fields)
    return solution, forcing - coupled
```

```python
import functools
import math

import jax
import jax.numpy as jnp
from jax import lax
from jax.experimental import pallas as pl
from jax.experimental.pallas import tpu as pltpu
from jax.sharding import PartitionSpec as P

SWEEPS = 2
LANES = 128
VMEM_BYTES = 67_000_000


def with_halo(block, sides, width):
    for axis, dim in sides:
        count = lax.axis_size(axis)
        forward = [(i, i + 1) for i in range(count - 1)]
        backward = [(target, source) for source, target in forward]
        low = lax.ppermute(
            lax.slice_in_dim(block, block.shape[dim] - width, None, axis=dim), axis, forward
        )
        high = lax.ppermute(lax.slice_in_dim(block, 0, width, axis=dim), axis, backward)
        block = jnp.concatenate([low, block, high], axis=dim)
    return block


def stencil_ext(coeff_ext, value_ext):
    coeff_mid = coeff_ext[1:-1]
    value_mid = value_ext[1:-1]
    coeff_side = jnp.pad(coeff_mid, ((0, 0), (1, 1)))
    value_side = jnp.pad(value_mid, ((0, 0), (1, 1)))
    result = 0.5 * (coeff_mid + coeff_ext[2:]) * (value_mid - value_ext[2:])
    result = result + 0.5 * (coeff_mid + coeff_ext[:-2]) * (value_mid - value_ext[:-2])
    result = result + 0.5 * (coeff_mid + coeff_side[:, 2:]) * (value_mid - value_side[:, 2:])
    result = result + 0.5 * (coeff_mid + coeff_side[:, :-2]) * (value_mid - value_side[:, :-2])
    return result


def face_sum_ext(coeff_ext):
    coeff_mid = coeff_ext[1:-1]
    coeff_side = jnp.pad(coeff_mid, ((0, 0), (1, 1)))
    result = 0.5 * (coeff_mid + coeff_ext[2:])
    result = result + 0.5 * (coeff_mid + coeff_ext[:-2])
    result = result + 0.5 * (coeff_mid + coeff_side[:, 2:])
    result = result + 0.5 * (coeff_mid + coeff_side[:, :-2])
    return result


def couple(gathered, sources, field_ids, weights, stacked_ext):

    def reader(reader_entry):
        source_rows, field_rows, weight_rows = reader_entry
        values = jnp.take(gathered, source_rows, axis=0)
        coeffs = jnp.take(stacked_ext, field_rows + 1, axis=0)
        fluxes = jax.vmap(stencil_ext)(coeffs, values)
        return jnp.sum(weight_rows[:, None, None] * fluxes, axis=0)

    return lax.map(reader, (sources, field_ids, weights))


def ranks(color, mode_dev, batches):
    grouped = color.reshape(-1, mode_dev)
    onehot = (grouped[:, :, None] == jnp.arange(batches, dtype=jnp.int32)[None, None, :]).astype(
        jnp.int32
    )
    earlier = jnp.cumsum(onehot, axis=1) - onehot
    return jnp.sum(onehot * earlier, axis=2).reshape(-1)


def by_batch(forcing, mean_field, coef_fields, color, pair_src, pair_field, pair_value):
    mode_dev = forcing.shape[0]
    batches = pair_src.shape[0]
    per_batch = mode_dev // batches
    stacked = jnp.concatenate([mean_field[None], coef_fields], axis=0)
    stacked_ext = with_halo(stacked, (("space", 1),), 1)
    diag_sum = face_sum_ext(stacked_ext[0])
    ranking = ranks(color, mode_dev, batches)
    owners = jnp.arange(color.shape[0], dtype=jnp.int32) // mode_dev
    pool_rows = owners * per_batch + ranking
    source_rows = jnp.take(pool_rows, pair_src, axis=0)
    offset = lax.axis_index("mode") * mode_dev
    local_color = lax.dynamic_slice_in_dim(color, offset, mode_dev)
    local_rank = lax.dynamic_slice_in_dim(ranking, offset, mode_dev)
    positions = jnp.arange(mode_dev, dtype=jnp.int32)
    slot_numbers = jnp.arange(per_batch, dtype=jnp.int32)
    solution = jnp.zeros(forcing.shape, jnp.float32)
    coupled = jnp.zeros(forcing.shape, jnp.float32)
    for sweep_idx in range(SWEEPS):
        for color_idx in range(batches):
            active = local_color == color_idx
            update = jnp.where(active[:, None, None], (forcing - coupled) / diag_sum, 0.0)
            solution = solution + update
            selected = (active[None, :] & (local_rank[None, :] == slot_numbers[:, None])).astype(
                jnp.int32
            )
            chosen = jnp.sum(positions[None, :] * selected, axis=1)
            own_update = jnp.take(update, chosen, axis=0)
            inner = lax.all_gather(own_update, "mode", axis=0, tiled=True)
            gathered = with_halo(inner, (("space", 1),), 1)
            coupled = coupled + couple(
                gathered,
                source_rows[color_idx],
                pair_field[color_idx],
                pair_value[color_idx],
                stacked_ext,
            )
    return (solution, forcing - coupled)


def split3(x):
    hi = x.astype(jnp.bfloat16)
    rest = x - hi.astype(jnp.float32)
    mid = rest.astype(jnp.bfloat16)
    low = (rest - mid.astype(jnp.float32)).astype(jnp.bfloat16)
    return hi, mid, low


def sweep_kernel(
    dims, f_ref, a_ref, inv_ref, w_ref, sol_ref, r_ref, ax, ay, ex, ey, dvx, dvy, w6, a6x, a6y
):
    batches, sources, modes, width, steps, cells, rows = dims
    blocks = modes // 8
    a = a_ref[...]
    for a6, shift in ((a6x, width), (a6y, 1)):
        hi, mid, low = split3(a + pltpu.roll(a, cells - shift, 1))
        a6[...] = jnp.concatenate([hi, mid, low, hi, mid, hi], axis=0)
    chunk = 2 * LANES
    for c in range(batches):
        hi, mid, low = split3(0.5 * w_ref[c])
        w6[...] = jnp.concatenate([hi, hi, hi, mid, mid, low], axis=1)

        @pl.loop(0, cells // chunk)
        def _(n):
            at = pl.ds(pl.multiple_of(n * chunk, chunk), chunk)
            ax[c, :, at] = jnp.dot(w6[...], a6x[:, at], preferred_element_type=jnp.float32)
            ay[c, :, at] = jnp.dot(w6[...], a6y[:, at], preferred_element_type=jnp.float32)

    r_ref[...] = f_ref[...]
    sol_ref[...] = jnp.zeros_like(sol_ref)
    ex[...] = jnp.zeros_like(ex)
    ey[...] = jnp.zeros_like(ey)
    for k in range(steps):
        c = k % batches
        mine = pl.ds(c * sources, sources)
        u = r_ref[mine, :] * inv_ref[...]
        sol_ref[mine, :] = sol_ref[mine, :] + u
        dvx[...] = u - pltpu.roll(u, cells - width, 1)
        dvy[...] = u - pltpu.roll(u, cells - 1, 1)
        first = (width * k) // LANES
        last = -(-(width * (rows - 1 - k)) // LANES)

        @pl.loop(first, last)
        def _(g):
            at = pl.ds(pl.multiple_of(g * LANES, LANES), LANES)
            for table, diff, out in ((ax, dvx, ex), (ay, dvy, ey)):
                sums = [None] * blocks
                for s in range(sources):
                    d = jnp.broadcast_to(diff[pl.ds(s, 1), at], (8, LANES))
                    for b in range(blocks):
                        term = table[c, pl.ds(s * modes + b * 8, 8), at] * d
                        sums[b] = term if s == 0 else sums[b] + term
                for b in range(blocks):
                    out[pl.ds(b * 8, 8), at] = sums[b]

        for b in range(blocks):
            some = pl.ds(b * 8, 8)
            x = ex[some, :]
            y = ey[some, :]
            div = (x - pltpu.roll(x, width, 1)) + (y - pltpu.roll(y, 1, 1))
            r_ref[some, :] = r_ref[some, :] - div


def patch_sizes(mesh, forcing, pair_src, coef_fields):
    owners = mesh.shape["mode"]
    modes, nx, ny = forcing.shape
    batches = pair_src.shape[0]
    depth = SWEEPS * batches
    slab = nx // mesh.shape["space"]
    cols = ny // owners
    width = cols + 2 * depth
    rows = slab + 2 * depth
    cells = -(-(rows * width) // (2 * LANES)) * 2 * LANES
    sources = modes // batches
    table = 2 * batches * sources * modes * cells * 4
    fits = (
        table + 12_000_000 < VMEM_BYTES
        and slab > depth
        and modes % 8 == 0
        and sources % 8 == 0
        and ny % owners == 0
        and coef_fields.shape[0] <= 40
    )
    return fits, (batches, sources, modes, width, depth, cells, rows)


def halo_rows(block, width):
    return with_halo(block, (("space", block.ndim - 2),), width)


def by_patch(dims, forcing, mean_field, coef_fields, color, pair_src, pair_field, pair_value):
    batches, sources, modes, width, depth, cells, rows = dims
    mode_dev, slab, ny = forcing.shape
    owners = modes // mode_dev
    per_batch = mode_dev // batches
    cols = ny // owners
    fields = coef_fields.shape[0]
    kpad = -(-fields // 8) * 8
    nz = pair_src.shape[2]
    me = lax.axis_index("mode")
    ranking = ranks(color, mode_dev, batches)
    mode_ids = jnp.arange(modes, dtype=jnp.int32)
    pool_rows = (mode_ids // mode_dev) * per_batch + ranking
    source_rows = jnp.sum(
        jnp.where(pair_src[..., None] == mode_ids, pool_rows, 0), axis=-1, dtype=jnp.int32
    )
    slot = color * per_batch + ranking
    local_slot = lax.dynamic_slice_in_dim(slot, me * mode_dev, mode_dev)
    slots = jnp.arange(mode_dev, dtype=jnp.int32)
    pick = slots[:, None] == local_slot[None, :]

    def reorder(x, table):
        return sum(
            jnp.where(
                table[:, j].reshape((-1,) + (1,) * (x.ndim - 1)), x[j][None], jnp.float32(0)
            )
            for j in range(mode_dev)
        )

    def windows(x):
        padded = jnp.pad(x, ((0, 0), (0, 0), (depth, depth)))
        return jnp.stack(
            [padded[:, :, m * cols : m * cols + width] for m in range(owners)], axis=0
        )

    ordered = reorder(forcing, pick)
    out = windows(halo_rows(ordered, depth)).reshape(owners, mode_dev, rows * width)
    out = jnp.pad(out, ((0, 0), (0, 0), (0, cells - rows * width)))
    key = (source_rows * kpad + pair_field).astype(jnp.float32)
    both = jnp.stack([key, pair_value], axis=0)
    both = reorder(both.transpose(2, 0, 1, 3), pick).reshape(-1)
    extra = -(-both.shape[0] // cells)
    both = jnp.pad(both, (0, extra * cells - both.shape[0])).reshape(1, extra, cells)
    out = jnp.concatenate([out, jnp.broadcast_to(both, (owners, extra, cells))], axis=1)
    got = lax.all_to_all(out, "mode", 0, 0, tiled=True)
    values = got[:, :mode_dev].reshape(owners, batches, per_batch, cells)
    values = values.transpose(1, 0, 2, 3).reshape(modes, cells)
    entries = got[:, mode_dev:].reshape(owners, extra * cells)
    entries = entries[:, : mode_dev * 2 * batches * nz].reshape(
        owners, batches, per_batch, 2, batches, nz
    )
    entries = entries.transpose(3, 4, 1, 0, 2, 5).reshape(2, batches, modes, nz)
    keys = entries[0].astype(jnp.int32)
    places = jnp.arange(sources * kpad, dtype=jnp.int32)
    dense = jnp.zeros((batches, modes, sources * kpad), jnp.float32)
    for z in range(nz):
        dense = dense + jnp.where(keys[:, :, z, None] == places, entries[1][:, :, z, None], 0.0)
    dense = dense.reshape(batches, modes, sources, kpad).transpose(0, 2, 1, 3)
    dense = dense.reshape(batches, sources * modes, kpad)

    def window(x, margin):
        padded = jnp.pad(x, ((0, 0), (0, 0), (margin, margin)))
        return lax.dynamic_slice_in_dim(padded, me * cols, cols + 2 * margin, axis=2)

    coef = halo_rows(window(coef_fields, depth), depth).reshape(fields, rows * width)
    coef = jnp.pad(coef, ((0, kpad - fields), (0, cells - rows * width)))
    mean = halo_rows(window(mean_field[None], depth + 1), depth + 1)[0]
    mid = mean[1:-1, 1:-1]
    diag = 0.5 * (
        4.0 * mid + mean[2:, 1:-1] + mean[:-2, 1:-1] + mean[1:-1, 2:] + mean[1:-1, :-2]
    )
    row_ids = lax.axis_index("space") * slab - depth + jnp.arange(rows)
    col_ids = me * cols - depth + jnp.arange(width)
    total_rows = slab * lax.axis_size("space")
    inside = ((row_ids >= 0) & (row_ids < total_rows))[:, None] & (
        (col_ids >= 0) & (col_ids < ny)
    )[None, :]
    inv = jnp.where(inside, 1.0 / jnp.where(inside, diag, 1.0), 0.0).reshape(1, rows * width)
    inv = jnp.pad(inv, ((0, 0), (0, cells - rows * width)))

    patch = jax.ShapeDtypeStruct((modes, cells), jnp.float32)
    vmem = pl.BlockSpec(memory_space=pltpu.VMEM)
    table = pltpu.VMEM((batches, sources * modes, cells), jnp.float32)
    state = pltpu.VMEM((modes, cells), jnp.float32)
    diff = pltpu.VMEM((sources, cells), jnp.float32)
    coef6 = pltpu.VMEM((6 * kpad, cells), jnp.bfloat16)
    sol, res = pl.pallas_call(
        functools.partial(sweep_kernel, dims),
        out_shape=(patch, patch),
        in_specs=[vmem] * 4,
        out_specs=(vmem, vmem),
        scratch_shapes=[
            table,
            table,
            state,
            state,
            diff,
            diff,
            pltpu.VMEM((sources * modes, 6 * kpad), jnp.bfloat16),
            coef6,
            coef6,
        ],
        compiler_params=pltpu.CompilerParams(vmem_limit_bytes=VMEM_BYTES),
        name="sweeps",
    )(values, coef, inv, dense)

    done = jnp.stack([sol, res], axis=0)[:, :, : rows * width]
    done = done.reshape(2, batches, owners, per_batch, rows, width)
    done = done[..., depth : depth + slab, depth : depth + cols]
    done = done.transpose(2, 0, 1, 3, 4, 5).reshape(owners, 2 * mode_dev * slab * cols)
    back = lax.all_to_all(done, "mode", 0, 0, tiled=True)
    back = back.reshape(owners, 2, mode_dev, slab, cols).transpose(2, 1, 3, 0, 4)
    back = reorder(back.reshape(mode_dev, 2, slab, ny), pick.T)
    return back[:, 0], back[:, 1]


def solution(mesh):
    specs = (
        P("mode", "space", None),
        P("space", None),
        P(None, "space", None),
        P(),
        P(None, "mode", None),
        P(None, "mode", None),
        P(None, "mode", None),
    )

    def whole(*args):
        fits, dims = patch_sizes(mesh, args[0], args[4], args[2])
        body = functools.partial(by_patch, dims) if fits else by_batch
        return jax.shard_map(
            body,
            mesh=mesh,
            in_specs=specs,
            out_specs=(P("mode", "space", None), P("mode", "space", None)),
            check_vma=False,
        )(*args)

    return whole
```

```python
import functools
import math

import jax
import jax.numpy as jnp
from jax import lax
from jax.experimental import pallas as pl
from jax.experimental.pallas import tpu as pltpu
from jax.sharding import PartitionSpec as P

SWEEPS = 2
LANES = 128
VMEM_BYTES = 67_000_000


def with_halo(block, sides, width):
    for axis, dim in sides:
        count = lax.axis_size(axis)
        forward = [(i, i + 1) for i in range(count - 1)]
        backward = [(target, source) for source, target in forward]
        low = lax.ppermute(
            lax.slice_in_dim(block, block.shape[dim] - width, None, axis=dim), axis, forward
        )
        high = lax.ppermute(lax.slice_in_dim(block, 0, width, axis=dim), axis, backward)
        block = jnp.concatenate([low, block, high], axis=dim)
    return block


def stencil_ext(coeff_ext, value_ext):
    coeff_mid = coeff_ext[1:-1]
    value_mid = value_ext[1:-1]
    coeff_side = jnp.pad(coeff_mid, ((0, 0), (1, 1)))
    value_side = jnp.pad(value_mid, ((0, 0), (1, 1)))
    result = 0.5 * (coeff_mid + coeff_ext[2:]) * (value_mid - value_ext[2:])
    result = result + 0.5 * (coeff_mid + coeff_ext[:-2]) * (value_mid - value_ext[:-2])
    result = result + 0.5 * (coeff_mid + coeff_side[:, 2:]) * (value_mid - value_side[:, 2:])
    result = result + 0.5 * (coeff_mid + coeff_side[:, :-2]) * (value_mid - value_side[:, :-2])
    return result


def face_sum_ext(coeff_ext):
    coeff_mid = coeff_ext[1:-1]
    coeff_side = jnp.pad(coeff_mid, ((0, 0), (1, 1)))
    result = 0.5 * (coeff_mid + coeff_ext[2:])
    result = result + 0.5 * (coeff_mid + coeff_ext[:-2])
    result = result + 0.5 * (coeff_mid + coeff_side[:, 2:])
    result = result + 0.5 * (coeff_mid + coeff_side[:, :-2])
    return result


def couple(gathered, sources, field_ids, weights, stacked_ext):

    def reader(reader_entry):
        source_rows, field_rows, weight_rows = reader_entry
        values = jnp.take(gathered, source_rows, axis=0)
        coeffs = jnp.take(stacked_ext, field_rows + 1, axis=0)
        fluxes = jax.vmap(stencil_ext)(coeffs, values)
        return jnp.sum(weight_rows[:, None, None] * fluxes, axis=0)

    return lax.map(reader, (sources, field_ids, weights))


def ranks(color, mode_dev, batches):
    grouped = color.reshape(-1, mode_dev)
    onehot = (grouped[:, :, None] == jnp.arange(batches, dtype=jnp.int32)[None, None, :]).astype(
        jnp.int32
    )
    earlier = jnp.cumsum(onehot, axis=1) - onehot
    return jnp.sum(onehot * earlier, axis=2).reshape(-1)


def by_batch(forcing, mean_field, coef_fields, color, pair_src, pair_field, pair_value):
    mode_dev = forcing.shape[0]
    batches = pair_src.shape[0]
    per_batch = mode_dev // batches
    stacked = jnp.concatenate([mean_field[None], coef_fields], axis=0)
    stacked_ext = with_halo(stacked, (("space", 1),), 1)
    diag_sum = face_sum_ext(stacked_ext[0])
    ranking = ranks(color, mode_dev, batches)
    owners = jnp.arange(color.shape[0], dtype=jnp.int32) // mode_dev
    pool_rows = owners * per_batch + ranking
    source_rows = jnp.take(pool_rows, pair_src, axis=0)
    offset = lax.axis_index("mode") * mode_dev
    local_color = lax.dynamic_slice_in_dim(color, offset, mode_dev)
    local_rank = lax.dynamic_slice_in_dim(ranking, offset, mode_dev)
    positions = jnp.arange(mode_dev, dtype=jnp.int32)
    slot_numbers = jnp.arange(per_batch, dtype=jnp.int32)
    solution = jnp.zeros(forcing.shape, jnp.float32)
    coupled = jnp.zeros(forcing.shape, jnp.float32)
    for sweep_idx in range(SWEEPS):
        for color_idx in range(batches):
            active = local_color == color_idx
            update = jnp.where(active[:, None, None], (forcing - coupled) / diag_sum, 0.0)
            solution = solution + update
            selected = (active[None, :] & (local_rank[None, :] == slot_numbers[:, None])).astype(
                jnp.int32
            )
            chosen = jnp.sum(positions[None, :] * selected, axis=1)
            own_update = jnp.take(update, chosen, axis=0)
            inner = lax.all_gather(own_update, "mode", axis=0, tiled=True)
            gathered = with_halo(inner, (("space", 1),), 1)
            coupled = coupled + couple(
                gathered,
                source_rows[color_idx],
                pair_field[color_idx],
                pair_value[color_idx],
                stacked_ext,
            )
    return (solution, forcing - coupled)


def split3(x):
    hi = x.astype(jnp.bfloat16).astype(jnp.float32)
    mid = (x - hi).astype(jnp.bfloat16).astype(jnp.float32)
    return hi, mid, x - hi - mid


def sweep_kernel(dims, win, pairs, cw, back, ax, ay, r, sol, ex, ey, dvx, dvy, w6, a6x, a6y,
                 allp, cbuf, inv, dense, send, recv, hsend, hrecv, csend, crecv):
    batches, sources, modes, width, steps, cells, rows, fields, nz, owners, slabs = dims
    mode_dev = modes // owners
    per_batch = mode_dev // batches
    blocks = modes // 8
    edge = width * steps
    core_cells = cells - 2 * edge
    me = lax.axis_index("mode")
    slab = lax.axis_index("space")
    low, mid_at, high = pl.ds(0, edge), pl.ds(edge, core_cells), pl.ds(cells - edge, edge)

    def owner_rows(o):
        return pl.ds(pl.multiple_of(o * mode_dev, mode_dev), mode_dev)

    def remote(src, dst, ssem, rsem, **where):
        return pltpu.make_async_remote_copy(
            src_ref=src, dst_ref=dst, send_sem=ssem, recv_sem=rsem, device_id=where,
            device_id_type=pl.DeviceIdType.MESH,
        )

    has_low, has_high = slab > 0, slab < slabs - 1
    barrier = pltpu.get_barrier_semaphore()
    for d in range(1, owners):
        pl.semaphore_signal(
            barrier, inc=1, device_id={"mode": lax.rem(me + d, owners)},
            device_id_type=pl.DeviceIdType.MESH,
        )
    for there, at in ((has_low, slab - 1), (has_high, slab + 1)):

        @pl.when(there)
        def _():
            pl.semaphore_signal(
                barrier, inc=1, device_id={"space": at}, device_id_type=pl.DeviceIdType.MESH
            )

    beside = has_low.astype(jnp.int32) + has_high.astype(jnp.int32)
    pl.semaphore_wait(barrier, owners - 1 + beside)

    def peer(d):
        return lax.rem(me + d, owners)

    def origin(d):
        return lax.rem(me + owners - d, owners)

    def pair_copy(d, o):
        return remote(pairs, allp.at[owner_rows(o)], send.at[0, d], recv.at[0, d], mode=peer(d))

    def value_copy(d, o):
        return remote(
            win.at[peer(d)], r.at[owner_rows(o), mid_at], send.at[1, d], recv.at[1, d],
            mode=peer(d),
        )

    def up_copy(d, o):
        return remote(
            r.at[owner_rows(o), pl.ds(core_cells, edge)], r.at[owner_rows(o), low],
            hsend.at[0, d], hrecv.at[0, d], space=slab + 1,
        )

    def down_copy(d, o):
        return remote(
            r.at[owner_rows(o), pl.ds(edge, edge)], r.at[owner_rows(o), high],
            hsend.at[1, d], hrecv.at[1, d], space=slab - 1,
        )

    def coef_up():
        return remote(
            cw.at[:, pl.ds(core_cells - edge, edge)], cbuf.at[:, low], csend.at[0], crecv.at[0],
            space=slab + 1,
        )

    def coef_down():
        return remote(
            cw.at[:, pl.ds(0, edge)], cbuf.at[:, high], csend.at[1], crecv.at[1], space=slab - 1
        )

    for d in range(1, owners):
        pair_copy(d, me).start()
    pl.when(has_high)(lambda: coef_up().start())
    pl.when(has_low)(lambda: coef_down().start())
    for d in range(1, owners):
        value_copy(d, me).start()

    allp[owner_rows(me), :] = pairs[...]
    r[owner_rows(me), mid_at] = win[me]
    cbuf[:, mid_at] = cw[...]
    for there, at in ((has_low, low), (has_high, high)):

        @pl.when(jnp.logical_not(there))
        def _():
            r[:, at] = jnp.zeros((modes, edge), jnp.float32)
            cbuf[:, at] = jnp.zeros((cbuf.shape[0], edge), jnp.float32)

    sol[...] = jnp.zeros_like(sol)
    ex[...] = jnp.zeros_like(ex)
    ey[...] = jnp.zeros_like(ey)

    pl.when(has_high)(lambda: coef_up().wait_send())
    pl.when(has_low)(lambda: coef_down().wait_send())
    pl.when(has_low)(lambda: coef_up().wait_recv())
    pl.when(has_high)(lambda: coef_down().wait_recv())
    a = cbuf[...]
    kpad = a.shape[0]
    for a6, shift in ((a6x, width), (a6y, 1)):
        parts = split3(0.5 * (a + pltpu.roll(a, cells - shift, 1)))
        hi, mid, rest = [x.astype(jnp.bfloat16) for x in parts]
        none = jnp.zeros_like(hi)
        a6[...] = jnp.concatenate([hi, mid, rest, hi, mid, hi, none, none], axis=0)
    extra = a[fields : fields + 4]
    place = lax.broadcasted_iota(jnp.int32, (1, cells), 1)
    centre, across = extra[1:2], extra[0:1]
    above = jnp.where(place < width, extra[2:3], pltpu.roll(centre, width, 1))
    below = jnp.where(
        place >= width * (rows - 1), extra[3:4], pltpu.roll(centre, cells - width, 1)
    )
    inside = across > 0.0
    diag = jnp.where(inside, 0.5 * (across + above + below), 1.0)
    inv[...] = jnp.where(inside, 1.0 / diag, 0.0)

    for d in range(1, owners):
        pair_copy(d, me).wait_send()
        pair_copy(d, me).wait_recv()

    chunk = 2 * LANES
    per_group = LANES // kpad
    lane = lax.broadcasted_iota(jnp.int32, (8, LANES), 1)
    lane_f = lane.astype(jnp.float32)
    value_lane = allp.shape[1] // 2

    def build(c):
        @pl.loop(0, blocks)
        def _(b):
            own = allp[pl.ds(pl.multiple_of(b * 8, 8), 8), :]
            sums = [jnp.zeros((8, LANES), jnp.float32)] * (sources // per_group)
            for z in range(nz):
                e = c * nz + z
                key = jnp.broadcast_to(own[:, e : e + 1], (8, LANES))
                val = jnp.broadcast_to(own[:, value_lane + e : value_lane + e + 1], (8, LANES))
                for g in range(sources // per_group):
                    sums[g] = sums[g] + jnp.where(key == lane_f + float(g * LANES), val, 0.0)
            for g in range(sources // per_group):
                for j in range(per_group):
                    one = jnp.where((lane >= j * kpad) & (lane < (j + 1) * kpad), sums[g], 0.0)
                    one = one + pltpu.roll(one, kpad, 1)
                    one = one + pltpu.roll(one, 2 * kpad, 1)
                    hi, mid, rest = split3(one)
                    first = jnp.where(lane < 3 * kpad, hi, mid)
                    second = jnp.where(lane < kpad, mid, jnp.where(lane < 2 * kpad, rest, 0.0))
                    at = pl.ds(pl.multiple_of((g * per_group + j) * modes + b * 8, 8), 8)
                    dense[at, pl.ds(0, LANES)] = first
                    dense[at, pl.ds(LANES, LANES)] = second

        w6[...] = dense[...].astype(jnp.bfloat16)

        @pl.loop(0, cells // chunk)
        def _(n):
            at = pl.ds(pl.multiple_of(n * chunk, chunk), chunk)
            ax[c, :, at] = jnp.dot(w6[...], a6x[:, at], preferred_element_type=jnp.float32)
            ay[c, :, at] = jnp.dot(w6[...], a6y[:, at], preferred_element_type=jnp.float32)

    build(0)
    for d in range(owners):
        if d:
            value_copy(d, me).wait_send()
            value_copy(d, me).wait_recv()
        pl.when(has_high)(lambda: up_copy(d, origin(d)).start())
        pl.when(has_low)(lambda: down_copy(d, origin(d)).start())
    for c in range(1, batches):
        build(c)
    for d in range(owners):
        pl.when(has_high)(lambda: up_copy(d, origin(d)).wait_send())
        pl.when(has_low)(lambda: down_copy(d, origin(d)).wait_send())
        pl.when(has_low)(lambda: up_copy(d, origin(d)).wait_recv())
        pl.when(has_high)(lambda: down_copy(d, origin(d)).wait_recv())

    def out_copy(which, src, d):
        return remote(
            src.at[owner_rows(peer(d)), mid_at], back.at[which, me], send.at[2 + which, d],
            recv.at[2 + which, d], mode=peer(d),
        )

    for k in range(steps):
        c = k % batches
        pieces = []
        for o in range(owners):
            mine = pl.ds(o * mode_dev + c * per_batch, per_batch)
            u = r[mine, :] * inv[...]
            sol[mine, :] = sol[mine, :] + u
            pieces.append(u)
        u = jnp.concatenate(pieces, axis=0)
        dvx[...] = u - pltpu.roll(u, cells - width, 1)
        dvy[...] = u - pltpu.roll(u, cells - 1, 1)
        if k == steps - 1:
            for d in range(1, owners):
                out_copy(0, sol, d).start()
        first = (width * k) // LANES
        last = -(-(width * (rows - 1 - k)) // LANES)

        @pl.loop(first, last)
        def _(g):
            at = pl.ds(pl.multiple_of(g * LANES, LANES), LANES)
            for table, diff, out in ((ax, dvx, ex), (ay, dvy, ey)):
                sums = [None] * blocks
                for s in range(sources):
                    dv = jnp.broadcast_to(diff[pl.ds(s, 1), at], (8, LANES))
                    for b in range(blocks):
                        term = table[c, pl.ds(s * modes + b * 8, 8), at] * dv
                        sums[b] = term if s == 0 else sums[b] + term
                for b in range(blocks):
                    out[pl.ds(b * 8, 8), at] = sums[b]

        for b in range(blocks):
            some = pl.ds(b * 8, 8)
            x = ex[some, :]
            y = ey[some, :]
            div = (x - pltpu.roll(x, width, 1)) + (y - pltpu.roll(y, 1, 1))
            r[some, :] = r[some, :] - div

    for d in range(1, owners):
        out_copy(1, r, d).start()
    for which, src in ((0, sol), (1, r)):
        back[which, me] = src[owner_rows(me), mid_at]
    for which, src in ((0, sol), (1, r)):
        for d in range(1, owners):
            out_copy(which, src, d).wait_send()
            out_copy(which, src, d).wait_recv()


def patch_sizes(mesh, forcing, pair_src, coef_fields):
    owners = mesh.shape["mode"]
    slabs = mesh.shape["space"]
    modes, nx, ny = forcing.shape
    batches = pair_src.shape[0]
    nz = pair_src.shape[2]
    fields = coef_fields.shape[0]
    depth = SWEEPS * batches
    slab = nx // slabs
    cols = ny // owners
    width = cols + 2 * depth
    rows = slab + 2 * depth
    cells = rows * width
    sources = modes // batches
    table = 2 * batches * sources * modes * cells * 4
    fits = (
        table + 12_000_000 < VMEM_BYTES
        and slab > depth
        and cells % (2 * LANES) == 0
        and (width * depth) % LANES == 0
        and modes == 8 * owners
        and sources % 8 == 0
        and ny % owners == 0
        and 24 < fields + 4 <= LANES // 4
        and batches * nz <= LANES
    )
    return fits, (batches, sources, modes, width, depth, cells, rows, fields, nz, owners, slabs)


def by_patch(dims, forcing, mean_field, coef_fields, color, pair_src, pair_field, pair_value):
    batches, sources, modes, width, depth, cells, rows, fields, nz, owners, slabs = dims
    mode_dev, slab, ny = forcing.shape
    per_batch = mode_dev // batches
    cols = ny // owners
    kpad = LANES // 4
    core_cells = slab * width
    me = lax.axis_index("mode")
    ranking = ranks(color, mode_dev, batches)
    mode_ids = jnp.arange(modes, dtype=jnp.int32)
    pool_rows = (mode_ids // mode_dev) * per_batch + ranking
    source_rows = jnp.sum(
        jnp.where(pair_src[..., None] == mode_ids, pool_rows, 0), axis=-1, dtype=jnp.int32
    )
    slot = color * per_batch + ranking
    local_slot = lax.dynamic_slice_in_dim(slot, me * mode_dev, mode_dev)
    slots = jnp.arange(mode_dev, dtype=jnp.int32)
    pick = slots[:, None] == local_slot[None, :]

    def reorder(x, table):
        return sum(
            jnp.where(
                table[:, j].reshape((-1,) + (1,) * (x.ndim - 1)), x[j][None], jnp.float32(0)
            )
            for j in range(mode_dev)
        )

    padded = jnp.pad(reorder(forcing, pick), ((0, 0), (0, 0), (depth, depth)))
    win = jnp.stack([padded[:, :, m * cols : m * cols + width] for m in range(owners)], axis=0)
    win = win.reshape(owners, mode_dev, core_cells)
    key = (source_rows * kpad + pair_field).astype(jnp.float32)
    both = jnp.stack([key, pair_value], axis=0).transpose(2, 0, 1, 3)
    both = reorder(both.reshape(mode_dev, 2, batches * nz), pick)
    both = jnp.pad(both, ((0, 0), (0, 0), (0, LANES - batches * nz)))
    both = both.reshape(mode_dev, 2 * LANES)

    side = jnp.pad(mean_field, ((0, 0), (1, 1)))
    across = 4.0 * mean_field + side[:, 2:] + side[:, :-2]
    later = jnp.pad(mean_field[1:], ((0, 1), (0, 0)))
    before = jnp.pad(mean_field[:-1], ((1, 0), (0, 0)))
    diag_parts = jnp.stack([across, mean_field, before, later], axis=0)
    coef = jnp.concatenate([coef_fields, diag_parts], axis=0)
    coef = jnp.pad(coef, ((0, kpad - fields - 4), (0, 0), (depth, depth)))
    coef = lax.dynamic_slice_in_dim(coef, me * cols, width, axis=2).reshape(kpad, core_cells)

    vmem = pl.BlockSpec(memory_space=pltpu.VMEM)
    table = pltpu.VMEM((batches, sources * modes, cells), jnp.float32)
    state = pltpu.VMEM((modes, cells), jnp.float32)
    diff = pltpu.VMEM((sources, cells), jnp.float32)
    coef6 = pltpu.VMEM((8 * kpad, cells), jnp.bfloat16)
    back = pl.pallas_call(
        functools.partial(sweep_kernel, dims),
        out_shape=jax.ShapeDtypeStruct((2, owners, mode_dev, core_cells), jnp.float32),
        in_specs=[vmem] * 3,
        out_specs=vmem,
        scratch_shapes=[
            table,
            table,
            state,
            state,
            state,
            state,
            diff,
            diff,
            pltpu.VMEM((sources * modes, 8 * kpad), jnp.bfloat16),
            coef6,
            coef6,
            pltpu.VMEM((modes, 2 * LANES), jnp.float32),
            pltpu.VMEM((kpad, cells), jnp.float32),
            pltpu.VMEM((1, cells), jnp.float32),
            pltpu.VMEM((sources * modes, 2 * LANES), jnp.float32),
            pltpu.SemaphoreType.DMA((4, owners)),
            pltpu.SemaphoreType.DMA((4, owners)),
            pltpu.SemaphoreType.DMA((2, owners)),
            pltpu.SemaphoreType.DMA((2, owners)),
            pltpu.SemaphoreType.DMA((2,)),
            pltpu.SemaphoreType.DMA((2,)),
        ],
        compiler_params=pltpu.CompilerParams(
            vmem_limit_bytes=VMEM_BYTES, collective_id=0, has_side_effects=True
        ),
        name="sweeps",
    )(win, both, coef)

    back = back.reshape(2, owners, mode_dev, slab, width)[..., depth : depth + cols]
    back = back.transpose(2, 0, 3, 1, 4).reshape(mode_dev, 2, slab, ny)
    back = reorder(back, pick.T)
    return back[:, 0], back[:, 1]


def solution(mesh):
    specs = (
        P("mode", "space", None),
        P("space", None),
        P(None, "space", None),
        P(),
        P(None, "mode", None),
        P(None, "mode", None),
        P(None, "mode", None),
    )

    def whole(*args):
        fits, dims = patch_sizes(mesh, args[0], args[4], args[2])
        body = functools.partial(by_patch, dims) if fits else by_batch
        return jax.shard_map(
            body,
            mesh=mesh,
            in_specs=specs,
            out_specs=(P("mode", "space", None), P("mode", "space", None)),
            check_vma=False,
        )(*args)

    return whole
```

```python
import functools
import math

import jax
import jax.numpy as jnp
from jax import lax
from jax.experimental import pallas as pl
from jax.experimental.pallas import tpu as pltpu
from jax.sharding import PartitionSpec as P

SWEEPS = 2
LANES = 128
VMEM_BYTES = 67_000_000


def with_halo(block, sides, width):
    for axis, dim in sides:
        count = lax.axis_size(axis)
        forward = [(i, i + 1) for i in range(count - 1)]
        backward = [(target, source) for source, target in forward]
        low = lax.ppermute(
            lax.slice_in_dim(block, block.shape[dim] - width, None, axis=dim), axis, forward
        )
        high = lax.ppermute(lax.slice_in_dim(block, 0, width, axis=dim), axis, backward)
        block = jnp.concatenate([low, block, high], axis=dim)
    return block


def stencil_ext(coeff_ext, value_ext):
    coeff_mid = coeff_ext[1:-1]
    value_mid = value_ext[1:-1]
    coeff_side = jnp.pad(coeff_mid, ((0, 0), (1, 1)))
    value_side = jnp.pad(value_mid, ((0, 0), (1, 1)))
    result = 0.5 * (coeff_mid + coeff_ext[2:]) * (value_mid - value_ext[2:])
    result = result + 0.5 * (coeff_mid + coeff_ext[:-2]) * (value_mid - value_ext[:-2])
    result = result + 0.5 * (coeff_mid + coeff_side[:, 2:]) * (value_mid - value_side[:, 2:])
    result = result + 0.5 * (coeff_mid + coeff_side[:, :-2]) * (value_mid - value_side[:, :-2])
    return result


def face_sum_ext(coeff_ext):
    coeff_mid = coeff_ext[1:-1]
    coeff_side = jnp.pad(coeff_mid, ((0, 0), (1, 1)))
    result = 0.5 * (coeff_mid + coeff_ext[2:])
    result = result + 0.5 * (coeff_mid + coeff_ext[:-2])
    result = result + 0.5 * (coeff_mid + coeff_side[:, 2:])
    result = result + 0.5 * (coeff_mid + coeff_side[:, :-2])
    return result


def couple(gathered, sources, field_ids, weights, stacked_ext):

    def reader(reader_entry):
        source_rows, field_rows, weight_rows = reader_entry
        values = jnp.take(gathered, source_rows, axis=0)
        coeffs = jnp.take(stacked_ext, field_rows + 1, axis=0)
        fluxes = jax.vmap(stencil_ext)(coeffs, values)
        return jnp.sum(weight_rows[:, None, None] * fluxes, axis=0)

    return lax.map(reader, (sources, field_ids, weights))


def ranks(color, mode_dev, batches):
    grouped = color.reshape(-1, mode_dev)
    onehot = (grouped[:, :, None] == jnp.arange(batches, dtype=jnp.int32)[None, None, :]).astype(
        jnp.int32
    )
    earlier = jnp.cumsum(onehot, axis=1) - onehot
    return jnp.sum(onehot * earlier, axis=2).reshape(-1)


def by_batch(forcing, mean_field, coef_fields, color, pair_src, pair_field, pair_value):
    mode_dev = forcing.shape[0]
    batches = pair_src.shape[0]
    per_batch = mode_dev // batches
    stacked = jnp.concatenate([mean_field[None], coef_fields], axis=0)
    stacked_ext = with_halo(stacked, (("space", 1),), 1)
    diag_sum = face_sum_ext(stacked_ext[0])
    ranking = ranks(color, mode_dev, batches)
    owners = jnp.arange(color.shape[0], dtype=jnp.int32) // mode_dev
    pool_rows = owners * per_batch + ranking
    source_rows = jnp.take(pool_rows, pair_src, axis=0)
    offset = lax.axis_index("mode") * mode_dev
    local_color = lax.dynamic_slice_in_dim(color, offset, mode_dev)
    local_rank = lax.dynamic_slice_in_dim(ranking, offset, mode_dev)
    positions = jnp.arange(mode_dev, dtype=jnp.int32)
    slot_numbers = jnp.arange(per_batch, dtype=jnp.int32)
    solution = jnp.zeros(forcing.shape, jnp.float32)
    coupled = jnp.zeros(forcing.shape, jnp.float32)
    for sweep_idx in range(SWEEPS):
        for color_idx in range(batches):
            active = local_color == color_idx
            update = jnp.where(active[:, None, None], (forcing - coupled) / diag_sum, 0.0)
            solution = solution + update
            selected = (active[None, :] & (local_rank[None, :] == slot_numbers[:, None])).astype(
                jnp.int32
            )
            chosen = jnp.sum(positions[None, :] * selected, axis=1)
            own_update = jnp.take(update, chosen, axis=0)
            inner = lax.all_gather(own_update, "mode", axis=0, tiled=True)
            gathered = with_halo(inner, (("space", 1),), 1)
            coupled = coupled + couple(
                gathered,
                source_rows[color_idx],
                pair_field[color_idx],
                pair_value[color_idx],
                stacked_ext,
            )
    return (solution, forcing - coupled)


def split3(x):
    hi = x.astype(jnp.bfloat16).astype(jnp.float32)
    mid = (x - hi).astype(jnp.bfloat16).astype(jnp.float32)
    return hi, mid, x - hi - mid


def sweep_kernel(dims, win, pairs, cw, back, ax, ay, r, sol, ex, ey, dvx, dvy, w6, a6x, a6y,
                 allp, cbuf, inv, dense, send, recv, hsend, hrecv, csend, crecv, packed):
    batches, sources, modes, width, steps, cells, rows, fields, nz, owners, slabs = dims
    mode_dev = modes // owners
    per_batch = mode_dev // batches
    blocks = modes // 8
    edge = width * steps
    core_cells = cells - 2 * edge
    me = lax.axis_index("mode")
    slab = lax.axis_index("space")
    low, mid_at, high = pl.ds(0, edge), pl.ds(edge, core_cells), pl.ds(cells - edge, edge)

    def owner_rows(o):
        return pl.ds(pl.multiple_of(o * mode_dev, mode_dev), mode_dev)

    def remote(src, dst, ssem, rsem, **where):
        return pltpu.make_async_remote_copy(
            src_ref=src, dst_ref=dst, send_sem=ssem, recv_sem=rsem, device_id=where,
            device_id_type=pl.DeviceIdType.MESH,
        )

    has_low, has_high = slab > 0, slab < slabs - 1
    barrier = pltpu.get_barrier_semaphore()
    for d in range(1, owners):
        pl.semaphore_signal(
            barrier, inc=1, device_id={"mode": lax.rem(me + d, owners)},
            device_id_type=pl.DeviceIdType.MESH,
        )
    for there, at in ((has_low, slab - 1), (has_high, slab + 1)):

        @pl.when(there)
        def _():
            pl.semaphore_signal(
                barrier, inc=1, device_id={"space": at}, device_id_type=pl.DeviceIdType.MESH
            )

    beside = has_low.astype(jnp.int32) + has_high.astype(jnp.int32)
    pl.semaphore_wait(barrier, owners - 1 + beside)

    def peer(d):
        return lax.rem(me + d, owners)

    def origin(d):
        return lax.rem(me + owners - d, owners)

    def pair_copy(d, o):
        return remote(pairs, allp.at[owner_rows(o)], send.at[0, d], recv.at[0, d], mode=peer(d))

    def value_copy(d, o):
        return remote(
            win.at[peer(d)], r.at[owner_rows(o), mid_at], send.at[1, d], recv.at[1, d],
            mode=peer(d),
        )

    def up_copy(d, o):
        return remote(
            r.at[owner_rows(o), pl.ds(core_cells, edge)], r.at[owner_rows(o), low],
            hsend.at[0, d], hrecv.at[0, d], space=slab + 1,
        )

    def down_copy(d, o):
        return remote(
            r.at[owner_rows(o), pl.ds(edge, edge)], r.at[owner_rows(o), high],
            hsend.at[1, d], hrecv.at[1, d], space=slab - 1,
        )

    def coef_up():
        return remote(
            cw.at[:, pl.ds(core_cells - edge, edge)], cbuf.at[:, low], csend.at[0], crecv.at[0],
            space=slab + 1,
        )

    def coef_down():
        return remote(
            cw.at[:, pl.ds(0, edge)], cbuf.at[:, high], csend.at[1], crecv.at[1], space=slab - 1
        )

    for d in range(1, owners):
        pair_copy(d, me).start()
    pl.when(has_high)(lambda: coef_up().start())
    pl.when(has_low)(lambda: coef_down().start())
    for d in range(1, owners):
        value_copy(d, me).start()

    allp[owner_rows(me), :] = pairs[...]
    r[owner_rows(me), mid_at] = win[me]
    cbuf[:, mid_at] = cw[...]
    for there, at in ((has_low, low), (has_high, high)):

        @pl.when(jnp.logical_not(there))
        def _():
            r[:, at] = jnp.zeros((modes, edge), jnp.float32)
            cbuf[:, at] = jnp.zeros((cbuf.shape[0], edge), jnp.float32)

    sol[...] = jnp.zeros_like(sol)
    ex[...] = jnp.zeros_like(ex)
    ey[...] = jnp.zeros_like(ey)

    pl.when(has_high)(lambda: coef_up().wait_send())
    pl.when(has_low)(lambda: coef_down().wait_send())
    pl.when(has_low)(lambda: coef_up().wait_recv())
    pl.when(has_high)(lambda: coef_down().wait_recv())
    a = cbuf[...]
    kpad = a.shape[0]
    for a6, shift in ((a6x, width), (a6y, 1)):
        parts = split3(0.5 * (a + pltpu.roll(a, cells - shift, 1)))
        hi, mid, rest = [x.astype(jnp.bfloat16) for x in parts]
        none = jnp.zeros_like(hi)
        a6[...] = jnp.concatenate([hi, mid, rest, hi, mid, hi, none, none], axis=0)
    extra = a[fields : fields + 4]
    place = lax.broadcasted_iota(jnp.int32, (1, cells), 1)
    centre, across = extra[1:2], extra[0:1]
    above = jnp.where(place < width, extra[2:3], pltpu.roll(centre, width, 1))
    below = jnp.where(
        place >= width * (rows - 1), extra[3:4], pltpu.roll(centre, cells - width, 1)
    )
    inside = across > 0.0
    diag = jnp.where(inside, 0.5 * (across + above + below), 1.0)
    inv[...] = jnp.where(inside, 1.0 / diag, 0.0)

    for d in range(1, owners):
        pair_copy(d, me).wait_send()
        pair_copy(d, me).wait_recv()

    chunk = 4 * LANES
    per_group = LANES // kpad
    lane = lax.broadcasted_iota(jnp.int32, (8, LANES), 1)
    lane_f = lane.astype(jnp.float32)
    value_lane = allp.shape[1] // 2

    def build(c):
        @pl.loop(0, blocks // 2)
        def _(pair):
            build_rows(c, 2 * pair)
            build_rows(c, 2 * pair + 1)

        w6[...] = dense[...].astype(jnp.bfloat16)

        @pl.loop(0, cells // chunk)
        def _(n):
            at = pl.ds(pl.multiple_of(n * chunk, chunk), chunk)
            for table, a6 in ((ax, a6x), (ay, a6y)):
                got = jnp.dot(w6[...], a6[:, at], preferred_element_type=jnp.float32)
                for q in range(chunk // LANES):
                    table[c, n * (chunk // LANES) + q] = got[:, q * LANES : (q + 1) * LANES]

    def build_rows(c, b):
        own = allp[pl.ds(pl.multiple_of(b * 8, 8), 8), :]
        sums = [jnp.zeros((8, LANES), jnp.float32)] * (sources // per_group)
        for z in range(nz):
            e = c * nz + z
            key = jnp.broadcast_to(own[:, e : e + 1], (8, LANES))
            val = jnp.broadcast_to(own[:, value_lane + e : value_lane + e + 1], (8, LANES))
            for g in range(sources // per_group):
                sums[g] = sums[g] + jnp.where(key == lane_f + float(g * LANES), val, 0.0)
        for g in range(sources // per_group):
            for j in range(per_group):
                one = jnp.where((lane >= j * kpad) & (lane < (j + 1) * kpad), sums[g], 0.0)
                one = one + pltpu.roll(one, kpad, 1)
                one = one + pltpu.roll(one, 2 * kpad, 1)
                hi, mid, rest = split3(one)
                first = jnp.where(lane < 3 * kpad, hi, mid)
                second = jnp.where(lane < kpad, mid, jnp.where(lane < 2 * kpad, rest, 0.0))
                at = pl.ds(pl.multiple_of((g * per_group + j) * modes + b * 8, 8), 8)
                dense[at, pl.ds(0, LANES)] = first
                dense[at, pl.ds(LANES, LANES)] = second

    build(0)
    for d in range(owners):
        if d:
            value_copy(d, me).wait_send()
            value_copy(d, me).wait_recv()
        pl.when(has_high)(lambda: up_copy(d, origin(d)).start())
        pl.when(has_low)(lambda: down_copy(d, origin(d)).start())
    for c in range(1, batches):
        build(c)
    for d in range(owners):
        pl.when(has_high)(lambda: up_copy(d, origin(d)).wait_send())
        pl.when(has_low)(lambda: down_copy(d, origin(d)).wait_send())
        pl.when(has_low)(lambda: up_copy(d, origin(d)).wait_recv())
        pl.when(has_high)(lambda: down_copy(d, origin(d)).wait_recv())

    cols = width - 2 * steps

    def pack(which, src):
        for b in range(blocks):
            x = src[pl.ds(b * 8, 8), mid_at]
            packed[which, pl.ds(b * 8, 8), :] = jnp.concatenate(
                [
                    x[:, q * width + steps : q * width + steps + cols]
                    for q in range(core_cells // width)
                ],
                axis=1,
            )

    def out_copy(which, d):
        return remote(
            packed.at[which, owner_rows(peer(d))], back.at[which, me], send.at[2 + which, d],
            recv.at[2 + which, d], mode=peer(d),
        )

    for k in range(steps):
        c = k % batches
        pieces = []
        for o in range(owners):
            mine = pl.ds(o * mode_dev + c * per_batch, per_batch)
            u = r[mine, :] * inv[...]
            sol[mine, :] = sol[mine, :] + u
            pieces.append(u)
        u = jnp.concatenate(pieces, axis=0)
        dvx[...] = u - pltpu.roll(u, cells - width, 1)
        dvy[...] = u - pltpu.roll(u, cells - 1, 1)
        if k == steps - 1:
            pack(0, sol)
            for d in range(1, owners):
                out_copy(0, d).start()
        first = (width * k) // LANES
        last = -(-(width * (rows - 1 - k)) // LANES)

        @pl.loop(first, last)
        def _(g):
            at = pl.ds(pl.multiple_of(g * LANES, LANES), LANES)
            for table, diff, out in ((ax, dvx, ex), (ay, dvy, ey)):
                sums = [None] * blocks
                for s in range(sources):
                    dv = jnp.broadcast_to(diff[pl.ds(s, 1), at], (8, LANES))
                    for b in range(blocks):
                        term = table[c, g, pl.ds(s * modes + b * 8, 8), :] * dv
                        sums[b] = term if s == 0 else sums[b] + term
                for b in range(blocks):
                    out[pl.ds(b * 8, 8), at] = sums[b]

        for b in range(blocks):
            some = pl.ds(b * 8, 8)
            x = ex[some, :]
            y = ey[some, :]
            div = (x - pltpu.roll(x, width, 1)) + (y - pltpu.roll(y, 1, 1))
            r[some, :] = r[some, :] - div

    pack(1, r)
    for d in range(1, owners):
        out_copy(1, d).start()
    for which in range(2):
        back[which, me] = packed[which, owner_rows(me), :]
    for which in range(2):
        for d in range(1, owners):
            out_copy(which, d).wait_send()
            out_copy(which, d).wait_recv()


def patch_sizes(mesh, forcing, pair_src, coef_fields):
    owners = mesh.shape["mode"]
    slabs = mesh.shape["space"]
    modes, nx, ny = forcing.shape
    batches = pair_src.shape[0]
    nz = pair_src.shape[2]
    fields = coef_fields.shape[0]
    depth = SWEEPS * batches
    slab = nx // slabs
    cols = ny // owners
    width = cols + 2 * depth
    rows = slab + 2 * depth
    cells = rows * width
    sources = modes // batches
    table = 2 * batches * sources * modes * cells * 4
    fits = (
        table + 12_000_000 < VMEM_BYTES
        and slab > depth
        and cells % (4 * LANES) == 0
        and (slab * cols) % LANES == 0
        and (width * depth) % LANES == 0
        and modes == 8 * owners
        and sources % 8 == 0
        and ny % owners == 0
        and 24 < fields + 4 <= LANES // 4
        and batches * nz <= LANES
    )
    return fits, (batches, sources, modes, width, depth, cells, rows, fields, nz, owners, slabs)


def by_patch(dims, forcing, mean_field, coef_fields, color, pair_src, pair_field, pair_value):
    batches, sources, modes, width, depth, cells, rows, fields, nz, owners, slabs = dims
    mode_dev, slab, ny = forcing.shape
    per_batch = mode_dev // batches
    cols = ny // owners
    kpad = LANES // 4
    core_cells = slab * width
    me = lax.axis_index("mode")
    ranking = ranks(color, mode_dev, batches)
    mode_ids = jnp.arange(modes, dtype=jnp.int32)
    pool_rows = (mode_ids // mode_dev) * per_batch + ranking
    source_rows = jnp.sum(
        jnp.where(pair_src[..., None] == mode_ids, pool_rows, 0), axis=-1, dtype=jnp.int32
    )
    slot = color * per_batch + ranking
    local_slot = lax.dynamic_slice_in_dim(slot, me * mode_dev, mode_dev)
    slots = jnp.arange(mode_dev, dtype=jnp.int32)
    pick = slots[:, None] == local_slot[None, :]

    def reorder(x, table):
        return sum(
            jnp.where(
                table[:, j].reshape((-1,) + (1,) * (x.ndim - 1)), x[j][None], jnp.float32(0)
            )
            for j in range(mode_dev)
        )

    padded = jnp.pad(reorder(forcing, pick), ((0, 0), (0, 0), (depth, depth)))
    win = jnp.stack([padded[:, :, m * cols : m * cols + width] for m in range(owners)], axis=0)
    win = win.reshape(owners, mode_dev, core_cells)
    key = (source_rows * kpad + pair_field).astype(jnp.float32)
    both = jnp.stack([key, pair_value], axis=0).transpose(2, 0, 1, 3)
    both = reorder(both.reshape(mode_dev, 2, batches * nz), pick)
    both = jnp.pad(both, ((0, 0), (0, 0), (0, LANES - batches * nz)))
    both = both.reshape(mode_dev, 2 * LANES)

    side = jnp.pad(mean_field, ((0, 0), (1, 1)))
    across = 4.0 * mean_field + side[:, 2:] + side[:, :-2]
    later = jnp.pad(mean_field[1:], ((0, 1), (0, 0)))
    before = jnp.pad(mean_field[:-1], ((1, 0), (0, 0)))
    diag_parts = jnp.stack([across, mean_field, before, later], axis=0)
    coef = jnp.concatenate([coef_fields, diag_parts], axis=0)
    coef = jnp.pad(coef, ((0, kpad - fields - 4), (0, 0), (depth, depth)))
    coef = lax.dynamic_slice_in_dim(coef, me * cols, width, axis=2).reshape(kpad, core_cells)

    vmem = pl.BlockSpec(memory_space=pltpu.VMEM)
    table = pltpu.VMEM((batches, cells // LANES, sources * modes, LANES), jnp.float32)
    state = pltpu.VMEM((modes, cells), jnp.float32)
    diff = pltpu.VMEM((sources, cells), jnp.float32)
    coef6 = pltpu.VMEM((8 * kpad, cells), jnp.bfloat16)
    back = pl.pallas_call(
        functools.partial(sweep_kernel, dims),
        out_shape=jax.ShapeDtypeStruct((2, owners, mode_dev, slab * cols), jnp.float32),
        in_specs=[vmem] * 3,
        out_specs=vmem,
        scratch_shapes=[
            table,
            table,
            state,
            state,
            state,
            state,
            diff,
            diff,
            pltpu.VMEM((sources * modes, 8 * kpad), jnp.bfloat16),
            coef6,
            coef6,
            pltpu.VMEM((modes, 2 * LANES), jnp.float32),
            pltpu.VMEM((kpad, cells), jnp.float32),
            pltpu.VMEM((1, cells), jnp.float32),
            pltpu.VMEM((sources * modes, 2 * LANES), jnp.float32),
            pltpu.SemaphoreType.DMA((4, owners)),
            pltpu.SemaphoreType.DMA((4, owners)),
            pltpu.SemaphoreType.DMA((2, owners)),
            pltpu.SemaphoreType.DMA((2, owners)),
            pltpu.SemaphoreType.DMA((2,)),
            pltpu.SemaphoreType.DMA((2,)),
            pltpu.VMEM((2, modes, slab * cols), jnp.float32),
        ],
        compiler_params=pltpu.CompilerParams(
            vmem_limit_bytes=VMEM_BYTES, collective_id=0, has_side_effects=True
        ),
        name="sweeps",
    )(win, both, coef)

    back = back.reshape(2, owners, mode_dev, slab, cols)
    back = back.transpose(2, 0, 3, 1, 4).reshape(mode_dev, 2, slab, ny)
    back = reorder(back, pick.T)
    return back[:, 0], back[:, 1]


def solution(mesh):
    specs = (
        P("mode", "space", None),
        P("space", None),
        P(None, "space", None),
        P(),
        P(None, "mode", None),
        P(None, "mode", None),
        P(None, "mode", None),
    )

    def whole(*args):
        fits, dims = patch_sizes(mesh, args[0], args[4], args[2])
        body = functools.partial(by_patch, dims) if fits else by_batch
        return jax.shard_map(
            body,
            mesh=mesh,
            in_specs=specs,
            out_specs=(P("mode", "space", None), P("mode", "space", None)),
            check_vma=False,
        )(*args)

    return whole
```

```python
import functools
import math

import jax
import jax.numpy as jnp
from jax import lax
from jax.experimental import pallas as pl
from jax.experimental.pallas import tpu as pltpu
from jax.sharding import PartitionSpec as P

SWEEPS = 2
LANES = 128
VMEM_BYTES = 67_000_000


def with_halo(block, sides, width):
    for axis, dim in sides:
        count = lax.axis_size(axis)
        forward = [(i, i + 1) for i in range(count - 1)]
        backward = [(target, source) for source, target in forward]
        low = lax.ppermute(
            lax.slice_in_dim(block, block.shape[dim] - width, None, axis=dim), axis, forward
        )
        high = lax.ppermute(lax.slice_in_dim(block, 0, width, axis=dim), axis, backward)
        block = jnp.concatenate([low, block, high], axis=dim)
    return block


def stencil_ext(coeff_ext, value_ext):
    coeff_mid = coeff_ext[1:-1]
    value_mid = value_ext[1:-1]
    coeff_side = jnp.pad(coeff_mid, ((0, 0), (1, 1)))
    value_side = jnp.pad(value_mid, ((0, 0), (1, 1)))
    result = 0.5 * (coeff_mid + coeff_ext[2:]) * (value_mid - value_ext[2:])
    result = result + 0.5 * (coeff_mid + coeff_ext[:-2]) * (value_mid - value_ext[:-2])
    result = result + 0.5 * (coeff_mid + coeff_side[:, 2:]) * (value_mid - value_side[:, 2:])
    result = result + 0.5 * (coeff_mid + coeff_side[:, :-2]) * (value_mid - value_side[:, :-2])
    return result


def face_sum_ext(coeff_ext):
    coeff_mid = coeff_ext[1:-1]
    coeff_side = jnp.pad(coeff_mid, ((0, 0), (1, 1)))
    result = 0.5 * (coeff_mid + coeff_ext[2:])
    result = result + 0.5 * (coeff_mid + coeff_ext[:-2])
    result = result + 0.5 * (coeff_mid + coeff_side[:, 2:])
    result = result + 0.5 * (coeff_mid + coeff_side[:, :-2])
    return result


def couple(gathered, sources, field_ids, weights, stacked_ext):

    def reader(reader_entry):
        source_rows, field_rows, weight_rows = reader_entry
        values = jnp.take(gathered, source_rows, axis=0)
        coeffs = jnp.take(stacked_ext, field_rows + 1, axis=0)
        fluxes = jax.vmap(stencil_ext)(coeffs, values)
        return jnp.sum(weight_rows[:, None, None] * fluxes, axis=0)

    return lax.map(reader, (sources, field_ids, weights))


def ranks(color, mode_dev, batches):
    grouped = color.reshape(-1, mode_dev)
    onehot = (grouped[:, :, None] == jnp.arange(batches, dtype=jnp.int32)[None, None, :]).astype(
        jnp.int32
    )
    earlier = jnp.cumsum(onehot, axis=1) - onehot
    return jnp.sum(onehot * earlier, axis=2).reshape(-1)


def by_batch(forcing, mean_field, coef_fields, color, pair_src, pair_field, pair_value):
    mode_dev = forcing.shape[0]
    batches = pair_src.shape[0]
    per_batch = mode_dev // batches
    stacked = jnp.concatenate([mean_field[None], coef_fields], axis=0)
    stacked_ext = with_halo(stacked, (("space", 1),), 1)
    diag_sum = face_sum_ext(stacked_ext[0])
    ranking = ranks(color, mode_dev, batches)
    owners = jnp.arange(color.shape[0], dtype=jnp.int32) // mode_dev
    pool_rows = owners * per_batch + ranking
    source_rows = jnp.take(pool_rows, pair_src, axis=0)
    offset = lax.axis_index("mode") * mode_dev
    local_color = lax.dynamic_slice_in_dim(color, offset, mode_dev)
    local_rank = lax.dynamic_slice_in_dim(ranking, offset, mode_dev)
    positions = jnp.arange(mode_dev, dtype=jnp.int32)
    slot_numbers = jnp.arange(per_batch, dtype=jnp.int32)
    solution = jnp.zeros(forcing.shape, jnp.float32)
    coupled = jnp.zeros(forcing.shape, jnp.float32)
    for sweep_idx in range(SWEEPS):
        for color_idx in range(batches):
            active = local_color == color_idx
            update = jnp.where(active[:, None, None], (forcing - coupled) / diag_sum, 0.0)
            solution = solution + update
            selected = (active[None, :] & (local_rank[None, :] == slot_numbers[:, None])).astype(
                jnp.int32
            )
            chosen = jnp.sum(positions[None, :] * selected, axis=1)
            own_update = jnp.take(update, chosen, axis=0)
            inner = lax.all_gather(own_update, "mode", axis=0, tiled=True)
            gathered = with_halo(inner, (("space", 1),), 1)
            coupled = coupled + couple(
                gathered,
                source_rows[color_idx],
                pair_field[color_idx],
                pair_value[color_idx],
                stacked_ext,
            )
    return (solution, forcing - coupled)


def split3(x):
    hi = x.astype(jnp.bfloat16).astype(jnp.float32)
    mid = (x - hi).astype(jnp.bfloat16).astype(jnp.float32)
    return hi, mid, x - hi - mid


def sweep_kernel(dims, win, pairs, cw, back, ax, ay, r, sol, ex, ey, dvx, dvy, w6, a6x, a6y,
                 allp, cbuf, inv, dense, send, recv, hsend, hrecv, csend, crecv, packed):
    batches, sources, modes, width, steps, cells, rows, fields, nz, owners, slabs = dims
    mode_dev = modes // owners
    per_batch = mode_dev // batches
    blocks = modes // 8
    edge = width * steps
    core_cells = cells - 2 * edge
    me = lax.axis_index("mode")
    slab = lax.axis_index("space")
    low, mid_at, high = pl.ds(0, edge), pl.ds(edge, core_cells), pl.ds(cells - edge, edge)

    def owner_rows(o):
        return pl.ds(pl.multiple_of(o * mode_dev, mode_dev), mode_dev)

    def remote(src, dst, ssem, rsem, **where):
        return pltpu.make_async_remote_copy(
            src_ref=src, dst_ref=dst, send_sem=ssem, recv_sem=rsem, device_id=where,
            device_id_type=pl.DeviceIdType.MESH,
        )

    has_low, has_high = slab > 0, slab < slabs - 1
    barrier = pltpu.get_barrier_semaphore()
    for d in range(1, owners):
        pl.semaphore_signal(
            barrier, inc=1, device_id={"mode": lax.rem(me + d, owners)},
            device_id_type=pl.DeviceIdType.MESH,
        )
    for there, at in ((has_low, slab - 1), (has_high, slab + 1)):

        @pl.when(there)
        def _():
            pl.semaphore_signal(
                barrier, inc=1, device_id={"space": at}, device_id_type=pl.DeviceIdType.MESH
            )

    def peer(d):
        return lax.rem(me + d, owners)

    def origin(d):
        return lax.rem(me + owners - d, owners)

    def pair_copy(d, o):
        return remote(pairs, allp.at[owner_rows(o)], send.at[0, d], recv.at[0, d], mode=peer(d))

    def value_copy(d, o):
        return remote(
            win.at[peer(d)], r.at[owner_rows(o), mid_at], send.at[1, d], recv.at[1, d],
            mode=peer(d),
        )

    def up_copy(d, o):
        return remote(
            r.at[owner_rows(o), pl.ds(core_cells, edge)], r.at[owner_rows(o), low],
            hsend.at[0, d], hrecv.at[0, d], space=slab + 1,
        )

    def down_copy(d, o):
        return remote(
            r.at[owner_rows(o), pl.ds(edge, edge)], r.at[owner_rows(o), high],
            hsend.at[1, d], hrecv.at[1, d], space=slab - 1,
        )

    def coef_up():
        return remote(
            cw.at[:, pl.ds(core_cells - edge, edge)], cbuf.at[:, low], csend.at[0], crecv.at[0],
            space=slab + 1,
        )

    def coef_down():
        return remote(
            cw.at[:, pl.ds(0, edge)], cbuf.at[:, high], csend.at[1], crecv.at[1], space=slab - 1
        )

    chunk = 4 * LANES
    kpad = cw.shape[0]
    per_group = LANES // kpad
    lane = lax.broadcasted_iota(jnp.int32, (8, LANES), 1)
    lane_f = lane.astype(jnp.float32)
    value_lane = allp.shape[1] // 2

    def build_rows(c, b):
        own = allp[pl.ds(pl.multiple_of(b * 8, 8), 8), :]
        sums = [jnp.zeros((8, LANES), jnp.float32)] * (sources // per_group)
        for z in range(nz):
            e = c * nz + z
            key = jnp.broadcast_to(own[:, e : e + 1], (8, LANES))
            val = jnp.broadcast_to(own[:, value_lane + e : value_lane + e + 1], (8, LANES))
            for g in range(sources // per_group):
                sums[g] = sums[g] + jnp.where(key == lane_f + float(g * LANES), val, 0.0)
        for g in range(sources // per_group):
            for j in range(per_group):
                one = jnp.where((lane >= j * kpad) & (lane < (j + 1) * kpad), sums[g], 0.0)
                one = one + pltpu.roll(one, kpad, 1)
                one = one + pltpu.roll(one, 2 * kpad, 1)
                hi, mid, rest = split3(one)
                first = jnp.where(lane < 3 * kpad, hi, mid)
                second = jnp.where(lane < kpad, mid, jnp.where(lane < 2 * kpad, rest, 0.0))
                at = pl.ds(pl.multiple_of((g * per_group + j) * modes + b * 8, 8), 8)
                dense[c, at, pl.ds(0, LANES)] = first
                dense[c, at, pl.ds(LANES, LANES)] = second

    allp[owner_rows(me), :] = pairs[...]
    r[owner_rows(me), mid_at] = win[me]
    cbuf[:, mid_at] = cw[...]
    for there, at in ((has_low, low), (has_high, high)):

        @pl.when(jnp.logical_not(there))
        def _():
            r[:, at] = jnp.zeros((modes, edge), jnp.float32)
            cbuf[:, at] = jnp.zeros((cbuf.shape[0], edge), jnp.float32)

    sol[...] = jnp.zeros_like(sol)
    ex[...] = jnp.zeros_like(ex)
    ey[...] = jnp.zeros_like(ey)

    for c in range(batches):
        build_rows(c, me)
    beside = has_low.astype(jnp.int32) + has_high.astype(jnp.int32)
    pl.semaphore_wait(barrier, owners - 1 + beside)

    for d in range(1, owners):
        pair_copy(d, me).start()
    pl.when(has_high)(lambda: coef_up().start())
    pl.when(has_low)(lambda: coef_down().start())
    for d in range(1, owners):
        value_copy(d, me).start()

    @pl.loop(1, owners)
    def _(d):
        pair_copy(d, me).wait_send()
        pair_copy(d, me).wait_recv()
        for c in range(batches):
            build_rows(c, origin(d))

    pl.when(has_high)(lambda: coef_up().wait_send())
    pl.when(has_low)(lambda: coef_down().wait_send())
    pl.when(has_low)(lambda: coef_up().wait_recv())
    pl.when(has_high)(lambda: coef_down().wait_recv())
    a = cbuf[...]
    for a6, shift in ((a6x, width), (a6y, 1)):
        parts = split3(0.5 * (a + pltpu.roll(a, cells - shift, 1)))
        hi, mid, rest = [x.astype(jnp.bfloat16) for x in parts]
        none = jnp.zeros_like(hi)
        a6[...] = jnp.concatenate([hi, mid, rest, hi, mid, hi, none, none], axis=0)
    extra = a[fields : fields + 4]
    place = lax.broadcasted_iota(jnp.int32, (1, cells), 1)
    centre, across = extra[1:2], extra[0:1]
    above = jnp.where(place < width, extra[2:3], pltpu.roll(centre, width, 1))
    below = jnp.where(
        place >= width * (rows - 1), extra[3:4], pltpu.roll(centre, cells - width, 1)
    )
    inside = across > 0.0
    diag = jnp.where(inside, 0.5 * (across + above + below), 1.0)
    inv[...] = jnp.where(inside, 1.0 / diag, 0.0)

    def build(c):
        w6[...] = dense[c].astype(jnp.bfloat16)

        @pl.loop(0, cells // chunk)
        def _(n):
            at = pl.ds(pl.multiple_of(n * chunk, chunk), chunk)
            for table, a6 in ((ax, a6x), (ay, a6y)):
                got = jnp.dot(w6[...], a6[:, at], preferred_element_type=jnp.float32)
                for q in range(chunk // LANES):
                    table[c, n * (chunk // LANES) + q] = got[:, q * LANES : (q + 1) * LANES]

    build(0)
    for d in range(owners):
        if d:
            value_copy(d, me).wait_send()
            value_copy(d, me).wait_recv()
        pl.when(has_high)(lambda: up_copy(d, origin(d)).start())
        pl.when(has_low)(lambda: down_copy(d, origin(d)).start())
    for c in range(1, batches):
        build(c)
    for d in range(owners):
        pl.when(has_high)(lambda: up_copy(d, origin(d)).wait_send())
        pl.when(has_low)(lambda: down_copy(d, origin(d)).wait_send())
        pl.when(has_low)(lambda: up_copy(d, origin(d)).wait_recv())
        pl.when(has_high)(lambda: down_copy(d, origin(d)).wait_recv())

    cols = width - 2 * steps

    def pack(which, src):
        for b in range(blocks):
            x = src[pl.ds(b * 8, 8), mid_at]
            packed[which, pl.ds(b * 8, 8), :] = jnp.concatenate(
                [
                    x[:, q * width + steps : q * width + steps + cols]
                    for q in range(core_cells // width)
                ],
                axis=1,
            )

    def out_copy(which, d):
        return remote(
            packed.at[which, owner_rows(peer(d))], back.at[which, me], send.at[2 + which, d],
            recv.at[2 + which, d], mode=peer(d),
        )

    for k in range(steps):
        c = k % batches
        pieces = []
        for o in range(owners):
            mine = pl.ds(o * mode_dev + c * per_batch, per_batch)
            u = r[mine, :] * inv[...]
            sol[mine, :] = sol[mine, :] + u
            pieces.append(u)
        u = jnp.concatenate(pieces, axis=0)
        dvx[...] = u - pltpu.roll(u, cells - width, 1)
        dvy[...] = u - pltpu.roll(u, cells - 1, 1)
        if k == steps - 1:
            pack(0, sol)
            for d in range(1, owners):
                out_copy(0, d).start()
        first = (width * k) // LANES
        last = -(-(width * (rows - 1 - k)) // LANES)

        @pl.loop(first, last)
        def _(g):
            at = pl.ds(pl.multiple_of(g * LANES, LANES), LANES)
            for table, diff, out in ((ax, dvx, ex), (ay, dvy, ey)):
                sums = [None] * blocks
                for s in range(sources):
                    dv = jnp.broadcast_to(diff[pl.ds(s, 1), at], (8, LANES))
                    for b in range(blocks):
                        term = table[c, g, pl.ds(s * modes + b * 8, 8), :] * dv
                        sums[b] = term if s == 0 else sums[b] + term
                for b in range(blocks):
                    out[pl.ds(b * 8, 8), at] = sums[b]

        for b in range(blocks):
            some = pl.ds(b * 8, 8)
            span = pl.ds(first * LANES, (last - first) * LANES)
            x = ex[some, span]
            y = ey[some, span]
            div = (x - pltpu.roll(x, width, 1)) + (y - pltpu.roll(y, 1, 1))
            r[some, span] = r[some, span] - div

    pack(1, r)
    for d in range(1, owners):
        out_copy(1, d).start()
    for which in range(2):
        back[which, me] = packed[which, owner_rows(me), :]
    for which in range(2):
        for d in range(1, owners):
            out_copy(which, d).wait_send()
            out_copy(which, d).wait_recv()


def patch_sizes(mesh, forcing, pair_src, coef_fields):
    owners = mesh.shape["mode"]
    slabs = mesh.shape["space"]
    modes, nx, ny = forcing.shape
    batches = pair_src.shape[0]
    nz = pair_src.shape[2]
    fields = coef_fields.shape[0]
    depth = SWEEPS * batches
    slab = nx // slabs
    cols = ny // owners
    width = cols + 2 * depth
    rows = slab + 2 * depth
    cells = rows * width
    sources = modes // batches
    table = 2 * batches * sources * modes * cells * 4
    fits = (
        table + 12_000_000 < VMEM_BYTES
        and slab > depth
        and cells % (4 * LANES) == 0
        and (slab * cols) % LANES == 0
        and (width * depth) % LANES == 0
        and modes == 8 * owners
        and sources % 8 == 0
        and ny % owners == 0
        and 24 < fields + 4 <= LANES // 4
        and batches * nz <= LANES
    )
    return fits, (batches, sources, modes, width, depth, cells, rows, fields, nz, owners, slabs)


def by_patch(dims, forcing, mean_field, coef_fields, color, pair_src, pair_field, pair_value):
    batches, sources, modes, width, depth, cells, rows, fields, nz, owners, slabs = dims
    mode_dev, slab, ny = forcing.shape
    per_batch = mode_dev // batches
    cols = ny // owners
    kpad = LANES // 4
    core_cells = slab * width
    me = lax.axis_index("mode")
    grouped = color.reshape(-1, mode_dev)
    ahead = jnp.arange(mode_dev)[None, :] < jnp.arange(mode_dev)[:, None]
    same = (grouped[:, :, None] == grouped[:, None, :]) & ahead[None]
    ranking = jnp.sum(same.astype(jnp.int32), axis=2).reshape(-1)
    mode_ids = jnp.arange(modes, dtype=jnp.int32)
    pool_rows = (mode_ids // mode_dev) * per_batch + ranking
    source_rows = jnp.sum(
        jnp.where(pair_src[..., None] == mode_ids, pool_rows, 0), axis=-1, dtype=jnp.int32
    )
    slot = color * per_batch + ranking
    local_slot = lax.dynamic_slice_in_dim(slot, me * mode_dev, mode_dev)
    slots = jnp.arange(mode_dev, dtype=jnp.int32)
    pick = slots[:, None] == local_slot[None, :]

    def reorder(x, table):
        return sum(
            jnp.where(
                table[:, j].reshape((-1,) + (1,) * (x.ndim - 1)), x[j][None], jnp.float32(0)
            )
            for j in range(mode_dev)
        )

    padded = jnp.pad(reorder(forcing, pick), ((0, 0), (0, 0), (depth, depth)))
    win = jnp.stack([padded[:, :, m * cols : m * cols + width] for m in range(owners)], axis=0)
    win = win.reshape(owners, mode_dev, core_cells)
    key = (source_rows * kpad + pair_field).astype(jnp.float32)
    both = jnp.stack([key, pair_value], axis=0).transpose(2, 0, 1, 3)
    both = reorder(both.reshape(mode_dev, 2, batches * nz), pick)
    both = jnp.pad(both, ((0, 0), (0, 0), (0, LANES - batches * nz)))
    both = both.reshape(mode_dev, 2 * LANES)

    side = jnp.pad(mean_field, ((0, 0), (1, 1)))
    across = 4.0 * mean_field + side[:, 2:] + side[:, :-2]
    later = jnp.pad(mean_field[1:], ((0, 1), (0, 0)))
    before = jnp.pad(mean_field[:-1], ((1, 0), (0, 0)))
    diag_parts = jnp.stack([across, mean_field, before, later], axis=0)
    coef = jnp.concatenate([coef_fields, diag_parts], axis=0)
    coef = jnp.pad(coef, ((0, kpad - fields - 4), (0, 0), (depth, depth)))
    coef = lax.dynamic_slice_in_dim(coef, me * cols, width, axis=2).reshape(kpad, core_cells)

    vmem = pl.BlockSpec(memory_space=pltpu.VMEM)
    table = pltpu.VMEM((batches, cells // LANES, sources * modes, LANES), jnp.float32)
    state = pltpu.VMEM((modes, cells), jnp.float32)
    diff = pltpu.VMEM((sources, cells), jnp.float32)
    coef6 = pltpu.VMEM((8 * kpad, cells), jnp.bfloat16)
    back = pl.pallas_call(
        functools.partial(sweep_kernel, dims),
        out_shape=jax.ShapeDtypeStruct((2, owners, mode_dev, slab * cols), jnp.float32),
        in_specs=[vmem] * 3,
        out_specs=vmem,
        scratch_shapes=[
            table,
            table,
            state,
            state,
            state,
            state,
            diff,
            diff,
            pltpu.VMEM((sources * modes, 8 * kpad), jnp.bfloat16),
            coef6,
            coef6,
            pltpu.VMEM((modes, 2 * LANES), jnp.float32),
            pltpu.VMEM((kpad, cells), jnp.float32),
            pltpu.VMEM((1, cells), jnp.float32),
            pltpu.VMEM((batches, sources * modes, 2 * LANES), jnp.float32),
            pltpu.SemaphoreType.DMA((4, owners)),
            pltpu.SemaphoreType.DMA((4, owners)),
            pltpu.SemaphoreType.DMA((2, owners)),
            pltpu.SemaphoreType.DMA((2, owners)),
            pltpu.SemaphoreType.DMA((2,)),
            pltpu.SemaphoreType.DMA((2,)),
            pltpu.VMEM((2, modes, slab * cols), jnp.float32),
        ],
        compiler_params=pltpu.CompilerParams(
            vmem_limit_bytes=VMEM_BYTES, collective_id=0, has_side_effects=True
        ),
        name="sweeps",
    )(win, both, coef)

    back = back.reshape(2, owners, mode_dev, slab, cols)
    back = back.transpose(2, 0, 3, 1, 4).reshape(mode_dev, 2, slab, ny)
    back = reorder(back, pick.T)
    return back[:, 0], back[:, 1]


def solution(mesh):
    specs = (
        P("mode", "space", None),
        P("space", None),
        P(None, "space", None),
        P(),
        P(None, "mode", None),
        P(None, "mode", None),
        P(None, "mode", None),
    )

    def whole(*args):
        fits, dims = patch_sizes(mesh, args[0], args[4], args[2])
        body = functools.partial(by_patch, dims) if fits else by_batch
        return jax.shard_map(
            body,
            mesh=mesh,
            in_specs=specs,
            out_specs=(P("mode", "space", None), P("mode", "space", None)),
            check_vma=False,
        )(*args)

    return whole
```

```python
import functools
import math

import jax
import jax.numpy as jnp
from jax import lax
from jax.experimental import pallas as pl
from jax.experimental.pallas import tpu as pltpu
from jax.sharding import PartitionSpec as P

SWEEPS = 2
LANES = 128
VMEM_BYTES = 67_000_000


def with_halo(block, sides, width):
    for axis, dim in sides:
        count = lax.axis_size(axis)
        forward = [(i, i + 1) for i in range(count - 1)]
        backward = [(target, source) for source, target in forward]
        low = lax.ppermute(
            lax.slice_in_dim(block, block.shape[dim] - width, None, axis=dim), axis, forward
        )
        high = lax.ppermute(lax.slice_in_dim(block, 0, width, axis=dim), axis, backward)
        block = jnp.concatenate([low, block, high], axis=dim)
    return block


def stencil_ext(coeff_ext, value_ext):
    coeff_mid = coeff_ext[1:-1]
    value_mid = value_ext[1:-1]
    coeff_side = jnp.pad(coeff_mid, ((0, 0), (1, 1)))
    value_side = jnp.pad(value_mid, ((0, 0), (1, 1)))
    result = 0.5 * (coeff_mid + coeff_ext[2:]) * (value_mid - value_ext[2:])
    result = result + 0.5 * (coeff_mid + coeff_ext[:-2]) * (value_mid - value_ext[:-2])
    result = result + 0.5 * (coeff_mid + coeff_side[:, 2:]) * (value_mid - value_side[:, 2:])
    result = result + 0.5 * (coeff_mid + coeff_side[:, :-2]) * (value_mid - value_side[:, :-2])
    return result


def face_sum_ext(coeff_ext):
    coeff_mid = coeff_ext[1:-1]
    coeff_side = jnp.pad(coeff_mid, ((0, 0), (1, 1)))
    result = 0.5 * (coeff_mid + coeff_ext[2:])
    result = result + 0.5 * (coeff_mid + coeff_ext[:-2])
    result = result + 0.5 * (coeff_mid + coeff_side[:, 2:])
    result = result + 0.5 * (coeff_mid + coeff_side[:, :-2])
    return result


def couple(gathered, sources, field_ids, weights, stacked_ext):

    def reader(reader_entry):
        source_rows, field_rows, weight_rows = reader_entry
        values = jnp.take(gathered, source_rows, axis=0)
        coeffs = jnp.take(stacked_ext, field_rows + 1, axis=0)
        fluxes = jax.vmap(stencil_ext)(coeffs, values)
        return jnp.sum(weight_rows[:, None, None] * fluxes, axis=0)

    return lax.map(reader, (sources, field_ids, weights))


def ranks(color, mode_dev, batches):
    grouped = color.reshape(-1, mode_dev)
    onehot = (grouped[:, :, None] == jnp.arange(batches, dtype=jnp.int32)[None, None, :]).astype(
        jnp.int32
    )
    earlier = jnp.cumsum(onehot, axis=1) - onehot
    return jnp.sum(onehot * earlier, axis=2).reshape(-1)


def by_batch(forcing, mean_field, coef_fields, color, pair_src, pair_field, pair_value):
    mode_dev = forcing.shape[0]
    batches = pair_src.shape[0]
    per_batch = mode_dev // batches
    stacked = jnp.concatenate([mean_field[None], coef_fields], axis=0)
    stacked_ext = with_halo(stacked, (("space", 1),), 1)
    diag_sum = face_sum_ext(stacked_ext[0])
    ranking = ranks(color, mode_dev, batches)
    owners = jnp.arange(color.shape[0], dtype=jnp.int32) // mode_dev
    pool_rows = owners * per_batch + ranking
    source_rows = jnp.take(pool_rows, pair_src, axis=0)
    offset = lax.axis_index("mode") * mode_dev
    local_color = lax.dynamic_slice_in_dim(color, offset, mode_dev)
    local_rank = lax.dynamic_slice_in_dim(ranking, offset, mode_dev)
    positions = jnp.arange(mode_dev, dtype=jnp.int32)
    slot_numbers = jnp.arange(per_batch, dtype=jnp.int32)
    solution = jnp.zeros(forcing.shape, jnp.float32)
    coupled = jnp.zeros(forcing.shape, jnp.float32)
    for sweep_idx in range(SWEEPS):
        for color_idx in range(batches):
            active = local_color == color_idx
            update = jnp.where(active[:, None, None], (forcing - coupled) / diag_sum, 0.0)
            solution = solution + update
            selected = (active[None, :] & (local_rank[None, :] == slot_numbers[:, None])).astype(
                jnp.int32
            )
            chosen = jnp.sum(positions[None, :] * selected, axis=1)
            own_update = jnp.take(update, chosen, axis=0)
            inner = lax.all_gather(own_update, "mode", axis=0, tiled=True)
            gathered = with_halo(inner, (("space", 1),), 1)
            coupled = coupled + couple(
                gathered,
                source_rows[color_idx],
                pair_field[color_idx],
                pair_value[color_idx],
                stacked_ext,
            )
    return (solution, forcing - coupled)


def split3(x):
    hi = x.astype(jnp.bfloat16).astype(jnp.float32)
    mid = (x - hi).astype(jnp.bfloat16).astype(jnp.float32)
    return hi, mid, x - hi - mid


def sweep_kernel(dims, win, pairs, cw, back, ax, ay, r, sol, ex, ey, dvx, dvy, w6, a6x, a6y,
                 allp, cbuf, inv, dense, send, recv, hsend, hrecv, csend, crecv, packed):
    batches, sources, modes, width, steps, cells, rows, fields, nz, owners, slabs = dims
    mode_dev = modes // owners
    per_batch = mode_dev // batches
    blocks = modes // 8
    edge = width * steps
    core_cells = cells - 2 * edge
    me = lax.axis_index("mode")
    slab = lax.axis_index("space")
    low, mid_at, high = pl.ds(0, edge), pl.ds(edge, core_cells), pl.ds(cells - edge, edge)

    def owner_rows(o):
        return pl.ds(pl.multiple_of(o * mode_dev, mode_dev), mode_dev)

    def remote(src, dst, ssem, rsem, **where):
        return pltpu.make_async_remote_copy(
            src_ref=src, dst_ref=dst, send_sem=ssem, recv_sem=rsem, device_id=where,
            device_id_type=pl.DeviceIdType.MESH,
        )

    has_low, has_high = slab > 0, slab < slabs - 1
    barrier = pltpu.get_barrier_semaphore()
    for d in range(1, owners):
        pl.semaphore_signal(
            barrier, inc=1, device_id={"mode": lax.rem(me + d, owners)},
            device_id_type=pl.DeviceIdType.MESH,
        )
    for there, at in ((has_low, slab - 1), (has_high, slab + 1)):

        @pl.when(there)
        def _():
            pl.semaphore_signal(
                barrier, inc=1, device_id={"space": at}, device_id_type=pl.DeviceIdType.MESH
            )

    def peer(d):
        return lax.rem(me + d, owners)

    def origin(d):
        return lax.rem(me + owners - d, owners)

    def pair_copy(d, o):
        return remote(pairs, allp.at[owner_rows(o)], send.at[0, d], recv.at[0, d], mode=peer(d))

    def value_copy(d, o):
        return remote(
            win.at[peer(d)], r.at[owner_rows(o), mid_at], send.at[1, d], recv.at[1, d],
            mode=peer(d),
        )

    def up_copy(d, o):
        return remote(
            r.at[owner_rows(o), pl.ds(core_cells, edge)], r.at[owner_rows(o), low],
            hsend.at[0, d], hrecv.at[0, d], space=slab + 1,
        )

    def down_copy(d, o):
        return remote(
            r.at[owner_rows(o), pl.ds(edge, edge)], r.at[owner_rows(o), high],
            hsend.at[1, d], hrecv.at[1, d], space=slab - 1,
        )

    def coef_up():
        return remote(
            cw.at[:, pl.ds(core_cells - edge, edge)], cbuf.at[:, low], csend.at[0], crecv.at[0],
            space=slab + 1,
        )

    def coef_down():
        return remote(
            cw.at[:, pl.ds(0, edge)], cbuf.at[:, high], csend.at[1], crecv.at[1], space=slab - 1
        )

    def groups_of(k):
        return (width * k) // LANES, -(-(width * (rows - 1 - k)) // LANES)

    kpad = cw.shape[0]
    per_group = LANES // kpad
    lane = lax.broadcasted_iota(jnp.int32, (8, LANES), 1)
    lane_f = lane.astype(jnp.float32)
    value_lane = allp.shape[1] // 2

    def build_rows(c, b):
        own = allp[pl.ds(pl.multiple_of(b * 8, 8), 8), :]
        sums = [jnp.zeros((8, LANES), jnp.float32)] * (sources // per_group)
        for z in range(nz):
            e = c * nz + z
            key = jnp.broadcast_to(own[:, e : e + 1], (8, LANES))
            val = jnp.broadcast_to(own[:, value_lane + e : value_lane + e + 1], (8, LANES))
            for g in range(sources // per_group):
                sums[g] = sums[g] + jnp.where(key == lane_f + float(g * LANES), val, 0.0)
        for g in range(sources // per_group):
            for j in range(per_group):
                one = jnp.where((lane >= j * kpad) & (lane < (j + 1) * kpad), sums[g], 0.0)
                one = one + pltpu.roll(one, kpad, 1)
                one = one + pltpu.roll(one, 2 * kpad, 1)
                hi, mid, rest = split3(one)
                first = jnp.where(lane < 3 * kpad, hi, mid)
                second = jnp.where(lane < kpad, mid, jnp.where(lane < 2 * kpad, rest, 0.0))
                at = pl.ds(pl.multiple_of((g * per_group + j) * modes + b * 8, 8), 8)
                dense[c, at, pl.ds(0, LANES)] = first
                dense[c, at, pl.ds(LANES, LANES)] = second

    allp[owner_rows(me), :] = pairs[...]
    r[owner_rows(me), mid_at] = win[me]
    cbuf[:, mid_at] = cw[...]
    for there, at in ((has_low, low), (has_high, high)):

        @pl.when(jnp.logical_not(there))
        def _():
            r[:, at] = jnp.zeros((modes, edge), jnp.float32)
            cbuf[:, at] = jnp.zeros((cbuf.shape[0], edge), jnp.float32)

    sol[...] = jnp.zeros_like(sol)
    ex[...] = jnp.zeros_like(ex)
    ey[...] = jnp.zeros_like(ey)

    for c in range(batches):
        build_rows(c, me)
    beside = has_low.astype(jnp.int32) + has_high.astype(jnp.int32)
    pl.semaphore_wait(barrier, owners - 1 + beside)

    for d in range(1, owners):
        pair_copy(d, me).start()
    pl.when(has_high)(lambda: coef_up().start())
    pl.when(has_low)(lambda: coef_down().start())
    for d in range(1, owners):
        value_copy(d, me).start()

    @pl.loop(1, owners)
    def _(d):
        pair_copy(d, me).wait_send()
        pair_copy(d, me).wait_recv()
        for c in range(batches):
            build_rows(c, origin(d))

    pl.when(has_high)(lambda: coef_up().wait_send())
    pl.when(has_low)(lambda: coef_down().wait_send())
    pl.when(has_low)(lambda: coef_up().wait_recv())
    pl.when(has_high)(lambda: coef_down().wait_recv())
    a = cbuf[...]
    for a6, shift in ((a6x, width), (a6y, 1)):
        parts = split3(0.5 * (a + pltpu.roll(a, cells - shift, 1)))
        hi, mid, rest = [x.astype(jnp.bfloat16) for x in parts]
        none = jnp.zeros_like(hi)
        a6[...] = jnp.concatenate([hi, mid, rest, hi, mid, hi, none, none], axis=0)
    extra = a[fields : fields + 4]
    place = lax.broadcasted_iota(jnp.int32, (1, cells), 1)
    centre, across = extra[1:2], extra[0:1]
    above = jnp.where(place < width, extra[2:3], pltpu.roll(centre, width, 1))
    below = jnp.where(
        place >= width * (rows - 1), extra[3:4], pltpu.roll(centre, cells - width, 1)
    )
    inside = across > 0.0
    diag = jnp.where(inside, 0.5 * (across + above + below), 1.0)
    inv[...] = jnp.where(inside, 1.0 / diag, 0.0)

    def build(c):
        w6[...] = dense[c].astype(jnp.bfloat16)

        first, last = groups_of(c)
        for start in range(first, last, 4):
            stop = min(start + 4, last)
            for table, a6 in ((ax, a6x), (ay, a6y)):
                got = jnp.dot(
                    w6[...], a6[:, start * LANES : stop * LANES],
                    preferred_element_type=jnp.float32,
                )
                for q in range(stop - start):
                    table[c, start + q] = got[:, q * LANES : (q + 1) * LANES]

    build(0)
    for d in range(owners):
        if d:
            value_copy(d, me).wait_send()
            value_copy(d, me).wait_recv()
        pl.when(has_high)(lambda: up_copy(d, origin(d)).start())
        pl.when(has_low)(lambda: down_copy(d, origin(d)).start())
    for c in range(1, batches):
        build(c)
    for d in range(owners):
        pl.when(has_high)(lambda: up_copy(d, origin(d)).wait_send())
        pl.when(has_low)(lambda: down_copy(d, origin(d)).wait_send())
        pl.when(has_low)(lambda: up_copy(d, origin(d)).wait_recv())
        pl.when(has_high)(lambda: down_copy(d, origin(d)).wait_recv())

    cols = width - 2 * steps

    def pack(which, src):
        for b in range(blocks):
            x = src[pl.ds(b * 8, 8), mid_at]
            packed[which, pl.ds(b * 8, 8), :] = jnp.concatenate(
                [
                    x[:, q * width + steps : q * width + steps + cols]
                    for q in range(core_cells // width)
                ],
                axis=1,
            )

    def out_copy(which, d):
        return remote(
            packed.at[which, owner_rows(peer(d))], back.at[which, me], send.at[2 + which, d],
            recv.at[2 + which, d], mode=peer(d),
        )

    for k in range(steps):
        c = k % batches
        first, last = groups_of(k)
        reach = -(-(width * (rows - k)) // LANES)
        size = (reach - first) * LANES
        span = pl.ds(first * LANES, size)
        scale = inv[:, span]
        row = lax.broadcasted_iota(jnp.int32, (mode_dev, size), 0)
        active = (row >= c * per_batch) & (row < (c + 1) * per_batch)
        for o in range(owners):
            mine = pl.ds(o * mode_dev, mode_dev)
            u = r[mine, span] * scale
            dvx[mine, span] = u - pltpu.roll(u, size - width, 1)
            dvy[mine, span] = u - pltpu.roll(u, size - 1, 1)
            sol[mine, span] = sol[mine, span] + jnp.where(active, u, 0.0)
        if k == steps - 1:
            pack(0, sol)
            for d in range(1, owners):
                out_copy(0, d).start()

        @pl.loop(first, last)
        def _(g):
            at = pl.ds(pl.multiple_of(g * LANES, LANES), LANES)
            for table, diff, out in ((ax, dvx, ex), (ay, dvy, ey)):
                sums = [None] * blocks
                for s in range(sources):
                    line = (s // per_batch) * mode_dev + c * per_batch + s % per_batch
                    dv = jnp.broadcast_to(diff[pl.ds(line, 1), at], (8, LANES))
                    for b in range(blocks):
                        term = table[c, g, pl.ds(s * modes + b * 8, 8), :] * dv
                        sums[b] = term if s == 0 else sums[b] + term
                for b in range(blocks):
                    out[pl.ds(b * 8, 8), at] = sums[b]

        for b in range(blocks):
            some = pl.ds(b * 8, 8)
            span = pl.ds(first * LANES, (last - first) * LANES)
            x = ex[some, span]
            y = ey[some, span]
            div = (x - pltpu.roll(x, width, 1)) + (y - pltpu.roll(y, 1, 1))
            r[some, span] = r[some, span] - div

    pack(1, r)
    for d in range(1, owners):
        out_copy(1, d).start()
    for which in range(2):
        back[which, me] = packed[which, owner_rows(me), :]
    for which in range(2):
        for d in range(1, owners):
            out_copy(which, d).wait_send()
            out_copy(which, d).wait_recv()


def patch_sizes(mesh, forcing, pair_src, coef_fields):
    owners = mesh.shape["mode"]
    slabs = mesh.shape["space"]
    modes, nx, ny = forcing.shape
    batches = pair_src.shape[0]
    nz = pair_src.shape[2]
    fields = coef_fields.shape[0]
    depth = SWEEPS * batches
    slab = nx // slabs
    cols = ny // owners
    width = cols + 2 * depth
    rows = slab + 2 * depth
    cells = rows * width
    sources = modes // batches
    table = 2 * batches * sources * modes * cells * 4
    fits = (
        table + 12_000_000 < VMEM_BYTES
        and slab > depth
        and cells % (4 * LANES) == 0
        and (slab * cols) % LANES == 0
        and (width * depth) % LANES == 0
        and modes == 8 * owners
        and sources % 8 == 0
        and ny % owners == 0
        and 24 < fields + 4 <= LANES // 4
        and batches * nz <= LANES
    )
    return fits, (batches, sources, modes, width, depth, cells, rows, fields, nz, owners, slabs)


def by_patch(dims, forcing, mean_field, coef_fields, color, pair_src, pair_field, pair_value):
    batches, sources, modes, width, depth, cells, rows, fields, nz, owners, slabs = dims
    mode_dev, slab, ny = forcing.shape
    per_batch = mode_dev // batches
    cols = ny // owners
    kpad = LANES // 4
    core_cells = slab * width
    me = lax.axis_index("mode")
    grouped = color.reshape(-1, mode_dev)
    ahead = jnp.arange(mode_dev)[None, :] < jnp.arange(mode_dev)[:, None]
    same = (grouped[:, :, None] == grouped[:, None, :]) & ahead[None]
    ranking = jnp.sum(same.astype(jnp.int32), axis=2).reshape(-1)
    mode_ids = jnp.arange(modes, dtype=jnp.int32)
    pool_rows = (mode_ids // mode_dev) * per_batch + ranking
    source_rows = jnp.sum(
        jnp.where(pair_src[..., None] == mode_ids, pool_rows, 0), axis=-1, dtype=jnp.int32
    )
    slot = color * per_batch + ranking
    local_slot = lax.dynamic_slice_in_dim(slot, me * mode_dev, mode_dev)
    slots = jnp.arange(mode_dev, dtype=jnp.int32)
    pick = slots[:, None] == local_slot[None, :]

    def reorder(x, table):
        return sum(
            jnp.where(
                table[:, j].reshape((-1,) + (1,) * (x.ndim - 1)), x[j][None], jnp.float32(0)
            )
            for j in range(mode_dev)
        )

    padded = jnp.pad(reorder(forcing, pick), ((0, 0), (0, 0), (depth, depth)))
    win = jnp.stack([padded[:, :, m * cols : m * cols + width] for m in range(owners)], axis=0)
    win = win.reshape(owners, mode_dev, core_cells)
    key = (source_rows * kpad + pair_field).astype(jnp.float32)
    both = jnp.stack([key, pair_value], axis=0).transpose(2, 0, 1, 3)
    both = reorder(both.reshape(mode_dev, 2, batches * nz), pick)
    both = jnp.pad(both, ((0, 0), (0, 0), (0, LANES - batches * nz)))
    both = both.reshape(mode_dev, 2 * LANES)

    side = jnp.pad(mean_field, ((0, 0), (1, 1)))
    across = 4.0 * mean_field + side[:, 2:] + side[:, :-2]
    later = jnp.pad(mean_field[1:], ((0, 1), (0, 0)))
    before = jnp.pad(mean_field[:-1], ((1, 0), (0, 0)))
    diag_parts = jnp.stack([across, mean_field, before, later], axis=0)
    coef = jnp.concatenate([coef_fields, diag_parts], axis=0)
    coef = jnp.pad(coef, ((0, kpad - fields - 4), (0, 0), (depth, depth)))
    coef = lax.dynamic_slice_in_dim(coef, me * cols, width, axis=2).reshape(kpad, core_cells)

    vmem = pl.BlockSpec(memory_space=pltpu.VMEM)
    table = pltpu.VMEM((batches, cells // LANES, sources * modes, LANES), jnp.float32)
    state = pltpu.VMEM((modes, cells), jnp.float32)
    coef6 = pltpu.VMEM((8 * kpad, cells), jnp.bfloat16)
    back = pl.pallas_call(
        functools.partial(sweep_kernel, dims),
        out_shape=jax.ShapeDtypeStruct((2, owners, mode_dev, slab * cols), jnp.float32),
        in_specs=[vmem] * 3,
        out_specs=vmem,
        scratch_shapes=[
            table,
            table,
            state,
            state,
            state,
            state,
            state,
            state,
            pltpu.VMEM((sources * modes, 8 * kpad), jnp.bfloat16),
            coef6,
            coef6,
            pltpu.VMEM((modes, 2 * LANES), jnp.float32),
            pltpu.VMEM((kpad, cells), jnp.float32),
            pltpu.VMEM((1, cells), jnp.float32),
            pltpu.VMEM((batches, sources * modes, 2 * LANES), jnp.float32),
            pltpu.SemaphoreType.DMA((4, owners)),
            pltpu.SemaphoreType.DMA((4, owners)),
            pltpu.SemaphoreType.DMA((2, owners)),
            pltpu.SemaphoreType.DMA((2, owners)),
            pltpu.SemaphoreType.DMA((2,)),
            pltpu.SemaphoreType.DMA((2,)),
            pltpu.VMEM((2, modes, slab * cols), jnp.float32),
        ],
        compiler_params=pltpu.CompilerParams(
            vmem_limit_bytes=VMEM_BYTES, collective_id=0, has_side_effects=True
        ),
        name="sweeps",
    )(win, both, coef)

    back = back.reshape(2, owners, mode_dev, slab, cols)
    back = back.transpose(2, 0, 3, 1, 4).reshape(mode_dev, 2, slab, ny)
    back = reorder(back, pick.T)
    return back[:, 0], back[:, 1]


def solution(mesh):
    specs = (
        P("mode", "space", None),
        P("space", None),
        P(None, "space", None),
        P(),
        P(None, "mode", None),
        P(None, "mode", None),
        P(None, "mode", None),
    )

    def whole(*args):
        fits, dims = patch_sizes(mesh, args[0], args[4], args[2])
        body = functools.partial(by_patch, dims) if fits else by_batch
        return jax.shard_map(
            body,
            mesh=mesh,
            in_specs=specs,
            out_specs=(P("mode", "space", None), P("mode", "space", None)),
            check_vma=False,
        )(*args)

    return whole
```

```python
import functools
import math

import jax
import jax.numpy as jnp
from jax import lax
from jax.experimental import pallas as pl
from jax.experimental.pallas import tpu as pltpu
from jax.sharding import PartitionSpec as P

SWEEPS = 2
LANES = 128
VMEM_BYTES = 67_000_000


def with_halo(block, sides, width):
    for axis, dim in sides:
        count = lax.axis_size(axis)
        forward = [(i, i + 1) for i in range(count - 1)]
        backward = [(target, source) for source, target in forward]
        low = lax.ppermute(
            lax.slice_in_dim(block, block.shape[dim] - width, None, axis=dim), axis, forward
        )
        high = lax.ppermute(lax.slice_in_dim(block, 0, width, axis=dim), axis, backward)
        block = jnp.concatenate([low, block, high], axis=dim)
    return block


def stencil_ext(coeff_ext, value_ext):
    coeff_mid = coeff_ext[1:-1]
    value_mid = value_ext[1:-1]
    coeff_side = jnp.pad(coeff_mid, ((0, 0), (1, 1)))
    value_side = jnp.pad(value_mid, ((0, 0), (1, 1)))
    result = 0.5 * (coeff_mid + coeff_ext[2:]) * (value_mid - value_ext[2:])
    result = result + 0.5 * (coeff_mid + coeff_ext[:-2]) * (value_mid - value_ext[:-2])
    result = result + 0.5 * (coeff_mid + coeff_side[:, 2:]) * (value_mid - value_side[:, 2:])
    result = result + 0.5 * (coeff_mid + coeff_side[:, :-2]) * (value_mid - value_side[:, :-2])
    return result


def face_sum_ext(coeff_ext):
    coeff_mid = coeff_ext[1:-1]
    coeff_side = jnp.pad(coeff_mid, ((0, 0), (1, 1)))
    result = 0.5 * (coeff_mid + coeff_ext[2:])
    result = result + 0.5 * (coeff_mid + coeff_ext[:-2])
    result = result + 0.5 * (coeff_mid + coeff_side[:, 2:])
    result = result + 0.5 * (coeff_mid + coeff_side[:, :-2])
    return result


def couple(gathered, sources, field_ids, weights, stacked_ext):

    def reader(reader_entry):
        source_rows, field_rows, weight_rows = reader_entry
        values = jnp.take(gathered, source_rows, axis=0)
        coeffs = jnp.take(stacked_ext, field_rows + 1, axis=0)
        fluxes = jax.vmap(stencil_ext)(coeffs, values)
        return jnp.sum(weight_rows[:, None, None] * fluxes, axis=0)

    return lax.map(reader, (sources, field_ids, weights))


def ranks(color, mode_dev, batches):
    grouped = color.reshape(-1, mode_dev)
    onehot = (grouped[:, :, None] == jnp.arange(batches, dtype=jnp.int32)[None, None, :]).astype(
        jnp.int32
    )
    earlier = jnp.cumsum(onehot, axis=1) - onehot
    return jnp.sum(onehot * earlier, axis=2).reshape(-1)


def by_batch(forcing, mean_field, coef_fields, color, pair_src, pair_field, pair_value):
    mode_dev = forcing.shape[0]
    batches = pair_src.shape[0]
    per_batch = mode_dev // batches
    stacked = jnp.concatenate([mean_field[None], coef_fields], axis=0)
    stacked_ext = with_halo(stacked, (("space", 1),), 1)
    diag_sum = face_sum_ext(stacked_ext[0])
    ranking = ranks(color, mode_dev, batches)
    owners = jnp.arange(color.shape[0], dtype=jnp.int32) // mode_dev
    pool_rows = owners * per_batch + ranking
    source_rows = jnp.take(pool_rows, pair_src, axis=0)
    offset = lax.axis_index("mode") * mode_dev
    local_color = lax.dynamic_slice_in_dim(color, offset, mode_dev)
    local_rank = lax.dynamic_slice_in_dim(ranking, offset, mode_dev)
    positions = jnp.arange(mode_dev, dtype=jnp.int32)
    slot_numbers = jnp.arange(per_batch, dtype=jnp.int32)
    solution = jnp.zeros(forcing.shape, jnp.float32)
    coupled = jnp.zeros(forcing.shape, jnp.float32)
    for sweep_idx in range(SWEEPS):
        for color_idx in range(batches):
            active = local_color == color_idx
            update = jnp.where(active[:, None, None], (forcing - coupled) / diag_sum, 0.0)
            solution = solution + update
            selected = (active[None, :] & (local_rank[None, :] == slot_numbers[:, None])).astype(
                jnp.int32
            )
            chosen = jnp.sum(positions[None, :] * selected, axis=1)
            own_update = jnp.take(update, chosen, axis=0)
            inner = lax.all_gather(own_update, "mode", axis=0, tiled=True)
            gathered = with_halo(inner, (("space", 1),), 1)
            coupled = coupled + couple(
                gathered,
                source_rows[color_idx],
                pair_field[color_idx],
                pair_value[color_idx],
                stacked_ext,
            )
    return (solution, forcing - coupled)


def split3(x):
    hi = x.astype(jnp.bfloat16).astype(jnp.float32)
    mid = (x - hi).astype(jnp.bfloat16).astype(jnp.float32)
    return hi, mid, x - hi - mid


def sweep_kernel(dims, win, pairs, cw, back, ax, ay, r, sol, ex, ey, dvx, dvy, w6, a6x, a6y,
                 allp, cbuf, inv, dense, send, recv, hsend, hrecv, csend, crecv, packed):
    batches, sources, modes, width, steps, cells, rows, fields, nz, owners, slabs = dims
    mode_dev = modes // owners
    per_batch = mode_dev // batches
    blocks = modes // 8
    edge = width * steps
    core_cells = cells - 2 * edge
    me = lax.axis_index("mode")
    slab = lax.axis_index("space")
    low, mid_at, high = pl.ds(0, edge), pl.ds(edge, core_cells), pl.ds(cells - edge, edge)

    def owner_rows(o):
        return pl.ds(pl.multiple_of(o * mode_dev, mode_dev), mode_dev)

    def remote(src, dst, ssem, rsem, **where):
        return pltpu.make_async_remote_copy(
            src_ref=src, dst_ref=dst, send_sem=ssem, recv_sem=rsem, device_id=where,
            device_id_type=pl.DeviceIdType.MESH,
        )

    has_low, has_high = slab > 0, slab < slabs - 1
    barrier = pltpu.get_barrier_semaphore()
    for d in range(1, owners):
        pl.semaphore_signal(
            barrier, inc=1, device_id={"mode": lax.rem(me + d, owners)},
            device_id_type=pl.DeviceIdType.MESH,
        )
    for there, at in ((has_low, slab - 1), (has_high, slab + 1)):

        @pl.when(there)
        def _():
            pl.semaphore_signal(
                barrier, inc=1, device_id={"space": at}, device_id_type=pl.DeviceIdType.MESH
            )

    def peer(d):
        return lax.rem(me + d, owners)

    def origin(d):
        return lax.rem(me + owners - d, owners)

    def pair_copy(d, o):
        return remote(pairs, allp.at[owner_rows(o)], send.at[0, d], recv.at[0, d], mode=peer(d))

    def value_copy(d, o):
        return remote(
            win.at[peer(d)], r.at[owner_rows(o), mid_at], send.at[1, d], recv.at[1, d],
            mode=peer(d),
        )

    def up_copy(d, o):
        return remote(
            r.at[owner_rows(o), pl.ds(core_cells, edge)], r.at[owner_rows(o), low],
            hsend.at[0, d], hrecv.at[0, d], space=slab + 1,
        )

    def down_copy(d, o):
        return remote(
            r.at[owner_rows(o), pl.ds(edge, edge)], r.at[owner_rows(o), high],
            hsend.at[1, d], hrecv.at[1, d], space=slab - 1,
        )

    def coef_up():
        return remote(
            cw.at[:, pl.ds(core_cells - edge, edge)], cbuf.at[:, low], csend.at[0], crecv.at[0],
            space=slab + 1,
        )

    def coef_down():
        return remote(
            cw.at[:, pl.ds(0, edge)], cbuf.at[:, high], csend.at[1], crecv.at[1], space=slab - 1
        )

    def groups_of(k):
        return (width * k) // LANES, -(-(width * (rows - 1 - k)) // LANES)

    kpad = cw.shape[0]
    per_group = LANES // kpad
    lane = lax.broadcasted_iota(jnp.int32, (8, LANES), 1)
    lane_f = lane.astype(jnp.float32)
    value_lane = allp.shape[1] // 2

    def build_rows(c, b):
        own = allp[pl.ds(pl.multiple_of(b * 8, 8), 8), :]
        sums = [jnp.zeros((8, LANES), jnp.float32)] * (sources // per_group)
        for z in range(nz):
            e = c * nz + z
            key = jnp.broadcast_to(own[:, e : e + 1], (8, LANES))
            val = jnp.broadcast_to(own[:, value_lane + e : value_lane + e + 1], (8, LANES))
            for g in range(sources // per_group):
                sums[g] = sums[g] + jnp.where(key == lane_f + float(g * LANES), val, 0.0)
        for g in range(sources // per_group):
            for j in range(per_group):
                one = jnp.where((lane >= j * kpad) & (lane < (j + 1) * kpad), sums[g], 0.0)
                one = one + pltpu.roll(one, kpad, 1)
                one = one + pltpu.roll(one, 2 * kpad, 1)
                hi, mid, rest = split3(one)
                first = jnp.where(lane < 3 * kpad, hi, mid)
                second = jnp.where(lane < kpad, mid, jnp.where(lane < 2 * kpad, rest, 0.0))
                at = pl.ds(pl.multiple_of((g * per_group + j) * modes + b * 8, 8), 8)
                dense[c, at, pl.ds(0, LANES)] = first
                dense[c, at, pl.ds(LANES, LANES)] = second

    allp[owner_rows(me), :] = pairs[...]
    r[owner_rows(me), mid_at] = win[me]
    cbuf[:, mid_at] = cw[...]
    for there, at in ((has_low, low), (has_high, high)):

        @pl.when(jnp.logical_not(there))
        def _():
            r[:, at] = jnp.zeros((modes, edge), jnp.float32)
            cbuf[:, at] = jnp.zeros((cbuf.shape[0], edge), jnp.float32)

    sol[...] = jnp.zeros_like(sol)
    ex[...] = jnp.zeros_like(ex)
    ey[...] = jnp.zeros_like(ey)

    for c in range(batches):
        build_rows(c, me)
    beside = has_low.astype(jnp.int32) + has_high.astype(jnp.int32)
    pl.semaphore_wait(barrier, owners - 1 + beside)

    for d in range(1, owners):
        pair_copy(d, me).start()
    pl.when(has_high)(lambda: coef_up().start())
    pl.when(has_low)(lambda: coef_down().start())
    for d in range(1, owners):
        value_copy(d, me).start()

    @pl.loop(1, owners)
    def _(d):
        pair_copy(d, me).wait_send()
        pair_copy(d, me).wait_recv()
        for c in range(batches):
            build_rows(c, origin(d))

    pl.when(has_high)(lambda: coef_up().wait_send())
    pl.when(has_low)(lambda: coef_down().wait_send())
    pl.when(has_low)(lambda: coef_up().wait_recv())
    pl.when(has_high)(lambda: coef_down().wait_recv())
    a = cbuf[...]
    for a6, shift in ((a6x, width), (a6y, 1)):
        parts = split3(0.5 * (a + pltpu.roll(a, cells - shift, 1)))
        hi, mid, rest = [x.astype(jnp.bfloat16) for x in parts]
        none = jnp.zeros_like(hi)
        a6[...] = jnp.concatenate([hi, mid, rest, hi, mid, hi, none, none], axis=0)
    extra = a[fields : fields + 4]
    place = lax.broadcasted_iota(jnp.int32, (1, cells), 1)
    centre, across = extra[1:2], extra[0:1]
    above = jnp.where(place < width, extra[2:3], pltpu.roll(centre, width, 1))
    below = jnp.where(
        place >= width * (rows - 1), extra[3:4], pltpu.roll(centre, cells - width, 1)
    )
    inside = across > 0.0
    diag = jnp.where(inside, 0.5 * (across + above + below), 1.0)
    inv[...] = jnp.where(inside, 1.0 / diag, 0.0)

    def build(c):
        w6[...] = dense[c].astype(jnp.bfloat16)

        first, last = groups_of(c)
        for start in range(first, last, 4):
            stop = min(start + 4, last)
            for table, a6 in ((ax, a6x), (ay, a6y)):
                got = jnp.dot(
                    w6[...], a6[:, start * LANES : stop * LANES],
                    preferred_element_type=jnp.float32,
                )
                for q in range(stop - start):
                    table[c, start + q] = got[:, q * LANES : (q + 1) * LANES]

    build(0)
    for d in range(owners):
        if d:
            value_copy(d, me).wait_send()
            value_copy(d, me).wait_recv()
        pl.when(has_high)(lambda: up_copy(d, origin(d)).start())
        pl.when(has_low)(lambda: down_copy(d, origin(d)).start())
    for c in range(1, batches):
        build(c)
    for d in range(owners):
        pl.when(has_high)(lambda: up_copy(d, origin(d)).wait_send())
        pl.when(has_low)(lambda: down_copy(d, origin(d)).wait_send())
        pl.when(has_low)(lambda: up_copy(d, origin(d)).wait_recv())
        pl.when(has_high)(lambda: down_copy(d, origin(d)).wait_recv())

    cols = width - 2 * steps

    def pack(which, src):
        for b in range(blocks):
            x = src[pl.ds(b * 8, 8), mid_at]
            packed[which, pl.ds(b * 8, 8), :] = jnp.concatenate(
                [
                    x[:, q * width + steps : q * width + steps + cols]
                    for q in range(core_cells // width)
                ],
                axis=1,
            )

    def out_copy(which, d):
        return remote(
            packed.at[which, owner_rows(peer(d))], back.at[which, me], send.at[2 + which, d],
            recv.at[2 + which, d], mode=peer(d),
        )

    for k in range(steps):
        c = k % batches
        first, last = groups_of(k)
        reach = -(-(width * (rows - k)) // LANES)
        size = (reach - first) * LANES
        span = pl.ds(first * LANES, size)
        scale = inv[:, span]
        row = lax.broadcasted_iota(jnp.int32, (mode_dev, size), 0)
        active = (row >= c * per_batch) & (row < (c + 1) * per_batch)
        for o in range(owners):
            mine = pl.ds(o * mode_dev, mode_dev)
            u = r[mine, span] * scale
            dvx[mine, span] = u - pltpu.roll(u, size - width, 1)
            dvy[mine, span] = u - pltpu.roll(u, size - 1, 1)
            sol[mine, span] = sol[mine, span] + jnp.where(active, u, 0.0)
        if k == steps - 1:
            pack(0, sol)
            for d in range(1, owners):
                out_copy(0, d).start()

        def accumulate(g):
            at = pl.ds(pl.multiple_of(g * LANES, LANES), LANES)
            for table, diff, out in ((ax, dvx, ex), (ay, dvy, ey)):
                sums = [None] * blocks
                for s in range(sources):
                    line = (s // per_batch) * mode_dev + c * per_batch + s % per_batch
                    dv = jnp.broadcast_to(diff[pl.ds(line, 1), at], (8, LANES))
                    for b in range(blocks):
                        term = table[c, g, pl.ds(s * modes + b * 8, 8), :] * dv
                        sums[b] = term if s == 0 else sums[b] + term
                for b in range(blocks):
                    out[pl.ds(b * 8, 8), at] = sums[b]

        @pl.loop(0, (last - first) // 2)
        def _(n):
            accumulate(first + 2 * n)
            accumulate(first + 2 * n + 1)

        if (last - first) % 2:
            accumulate(last - 1)

        for b in range(blocks):
            some = pl.ds(b * 8, 8)
            span = pl.ds(first * LANES, (last - first) * LANES)
            x = ex[some, span]
            y = ey[some, span]
            div = (x - pltpu.roll(x, width, 1)) + (y - pltpu.roll(y, 1, 1))
            r[some, span] = r[some, span] - div

    pack(1, r)
    for d in range(1, owners):
        out_copy(1, d).start()
    for which in range(2):
        back[which, me] = packed[which, owner_rows(me), :]
    for which in range(2):
        for d in range(1, owners):
            out_copy(which, d).wait_send()
            out_copy(which, d).wait_recv()


def patch_sizes(mesh, forcing, pair_src, coef_fields):
    owners = mesh.shape["mode"]
    slabs = mesh.shape["space"]
    modes, nx, ny = forcing.shape
    batches = pair_src.shape[0]
    nz = pair_src.shape[2]
    fields = coef_fields.shape[0]
    depth = SWEEPS * batches
    slab = nx // slabs
    cols = ny // owners
    width = cols + 2 * depth
    rows = slab + 2 * depth
    cells = rows * width
    sources = modes // batches
    table = 2 * batches * sources * modes * cells * 4
    fits = (
        table + 12_000_000 < VMEM_BYTES
        and slab > depth
        and cells % (4 * LANES) == 0
        and (slab * cols) % LANES == 0
        and (width * depth) % LANES == 0
        and modes == 8 * owners
        and sources % 8 == 0
        and ny % owners == 0
        and 24 < fields + 4 <= LANES // 4
        and batches * nz <= LANES
    )
    return fits, (batches, sources, modes, width, depth, cells, rows, fields, nz, owners, slabs)


def by_patch(dims, forcing, mean_field, coef_fields, color, pair_src, pair_field, pair_value):
    batches, sources, modes, width, depth, cells, rows, fields, nz, owners, slabs = dims
    mode_dev, slab, ny = forcing.shape
    per_batch = mode_dev // batches
    cols = ny // owners
    kpad = LANES // 4
    core_cells = slab * width
    me = lax.axis_index("mode")
    grouped = color.reshape(-1, mode_dev)
    ahead = jnp.arange(mode_dev)[None, :] < jnp.arange(mode_dev)[:, None]
    same = (grouped[:, :, None] == grouped[:, None, :]) & ahead[None]
    ranking = jnp.sum(same.astype(jnp.int32), axis=2).reshape(-1)
    mode_ids = jnp.arange(modes, dtype=jnp.int32)
    pool_rows = (mode_ids // mode_dev) * per_batch + ranking
    source_rows = jnp.sum(
        jnp.where(pair_src[..., None] == mode_ids, pool_rows, 0), axis=-1, dtype=jnp.int32
    )
    slot = color * per_batch + ranking
    local_slot = lax.dynamic_slice_in_dim(slot, me * mode_dev, mode_dev)
    slots = jnp.arange(mode_dev, dtype=jnp.int32)
    pick = slots[:, None] == local_slot[None, :]

    def reorder(x, table):
        return sum(
            jnp.where(
                table[:, j].reshape((-1,) + (1,) * (x.ndim - 1)), x[j][None], jnp.float32(0)
            )
            for j in range(mode_dev)
        )

    padded = jnp.pad(reorder(forcing, pick), ((0, 0), (0, 0), (depth, depth)))
    win = jnp.stack([padded[:, :, m * cols : m * cols + width] for m in range(owners)], axis=0)
    win = win.reshape(owners, mode_dev, core_cells)
    key = (source_rows * kpad + pair_field).astype(jnp.float32)
    both = jnp.stack([key, pair_value], axis=0).transpose(2, 0, 1, 3)
    both = reorder(both.reshape(mode_dev, 2, batches * nz), pick)
    both = jnp.pad(both, ((0, 0), (0, 0), (0, LANES - batches * nz)))
    both = both.reshape(mode_dev, 2 * LANES)

    side = jnp.pad(mean_field, ((0, 0), (1, 1)))
    across = 4.0 * mean_field + side[:, 2:] + side[:, :-2]
    later = jnp.pad(mean_field[1:], ((0, 1), (0, 0)))
    before = jnp.pad(mean_field[:-1], ((1, 0), (0, 0)))
    diag_parts = jnp.stack([across, mean_field, before, later], axis=0)
    coef = jnp.concatenate([coef_fields, diag_parts], axis=0)
    coef = jnp.pad(coef, ((0, kpad - fields - 4), (0, 0), (depth, depth)))
    coef = lax.dynamic_slice_in_dim(coef, me * cols, width, axis=2).reshape(kpad, core_cells)

    vmem = pl.BlockSpec(memory_space=pltpu.VMEM)
    table = pltpu.VMEM((batches, cells // LANES, sources * modes, LANES), jnp.float32)
    state = pltpu.VMEM((modes, cells), jnp.float32)
    coef6 = pltpu.VMEM((8 * kpad, cells), jnp.bfloat16)
    back = pl.pallas_call(
        functools.partial(sweep_kernel, dims),
        out_shape=jax.ShapeDtypeStruct((2, owners, mode_dev, slab * cols), jnp.float32),
        in_specs=[vmem] * 3,
        out_specs=vmem,
        scratch_shapes=[
            table,
            table,
            state,
            state,
            state,
            state,
            state,
            state,
            pltpu.VMEM((sources * modes, 8 * kpad), jnp.bfloat16),
            coef6,
            coef6,
            pltpu.VMEM((modes, 2 * LANES), jnp.float32),
            pltpu.VMEM((kpad, cells), jnp.float32),
            pltpu.VMEM((1, cells), jnp.float32),
            pltpu.VMEM((batches, sources * modes, 2 * LANES), jnp.float32),
            pltpu.SemaphoreType.DMA((4, owners)),
            pltpu.SemaphoreType.DMA((4, owners)),
            pltpu.SemaphoreType.DMA((2, owners)),
            pltpu.SemaphoreType.DMA((2, owners)),
            pltpu.SemaphoreType.DMA((2,)),
            pltpu.SemaphoreType.DMA((2,)),
            pltpu.VMEM((2, modes, slab * cols), jnp.float32),
        ],
        compiler_params=pltpu.CompilerParams(
            vmem_limit_bytes=VMEM_BYTES, collective_id=0, has_side_effects=True
        ),
        name="sweeps",
    )(win, both, coef)

    back = back.reshape(2, owners, mode_dev, slab, cols)
    back = back.transpose(2, 0, 3, 1, 4).reshape(mode_dev, 2, slab, ny)
    back = reorder(back, pick.T)
    return back[:, 0], back[:, 1]


def solution(mesh):
    specs = (
        P("mode", "space", None),
        P("space", None),
        P(None, "space", None),
        P(),
        P(None, "mode", None),
        P(None, "mode", None),
        P(None, "mode", None),
    )

    def whole(*args):
        fits, dims = patch_sizes(mesh, args[0], args[4], args[2])
        body = functools.partial(by_patch, dims) if fits else by_batch
        return jax.shard_map(
            body,
            mesh=mesh,
            in_specs=specs,
            out_specs=(P("mode", "space", None), P("mode", "space", None)),
            check_vma=False,
        )(*args)

    return whole
```
